32 devices in a mesh: chan: 4 (over y, core), seq: 8 (over z, x).
Axes of the slice: x: 2, y: 2, z: 4, core: 2. Of those that a mesh axis runs over, the one named last changes fastest.
Arguments:
- query_proj: bfloat16 [65536, 2048], P('seq', 'chan'), may hold values from -6 to 6
- key_proj: bfloat16 [65536, 2048], P('seq', 'chan'), may hold values from -6 to 6
- value_proj: bfloat16 [65536, 2048], P('seq', 'chan'), may hold values from -6 to 6
- short_taps: float32 [3, 3, 2048], P(None, None, 'chan'), may hold values from -3.5 to 3.5
- skip_gain: float32 [2048], P('chan'), may hold values from -6 to 6
- long_filter: float32 [4, 65536], P('chan', 'seq'), may hold values from -0.0234375 to 0.0234375
Outputs:
- mixed: float32 [65536, 2048], P('seq', 'chan')
The draws below stay inside these ranges and needn't reach their ends.
All inputs are finite; a program needn't handle non-finite values.
Results may differ from the reference program's by a relative error of at most 0.0003.
Values may be sent and summed in bfloat16 or wider, within the bound.
No kernel may reach another device: no remote copies, remote signals or barrier semaphores. Data moves between devices by JAX's collectives and lax.ppermute only.
A program may use at most 256 MiB of HBM per device.

```python
import jax
import jax.numpy as jnp

D = 2048
GROUP_W = 512
GROUPS = 4
SEQ = 65536


def block_levels(key, shape, split, least, largest):
    factor_of, own = 1.0, jax.random.fold_in(key, 6)
    for position, blocks in split:
        steps = jnp.exp(jax.random.uniform(jax.random.fold_in(own, position), (blocks,), jnp.float32, least / len(split), largest / len(split)))
        factor_of = factor_of * jnp.repeat(steps, shape[position] // blocks).reshape([-1 if axis == position else 1 for axis in range(len(shape))])
    return factor_of


def gaussian(stream_key, extent, width, most, pieces=(), kind=jnp.bfloat16):
    values = width * jax.random.normal(stream_key, extent, jnp.float32)
    if pieces:
        values = values * block_levels(stream_key, extent, pieces, -0.22, 0.18)
    return jnp.clip(values, -most, most).astype(kind)


def setup_inputs(seed: int = 0) -> dict:
    arg_keys = jax.random.split(jax.random.key(seed), 7)
    query_proj = gaussian(arg_keys[0], (SEQ, D), 1.0, 6.0, ((0, 8), (1, 4)))
    key_proj = gaussian(arg_keys[1], (SEQ, D), 1.0, 6.0, ((0, 8), (1, 4)))
    value_proj = gaussian(arg_keys[2], (SEQ, D), 1.0, 6.0, ((0, 8), (1, 4)))
    short_taps = gaussian(arg_keys[3], (3, 3, D), 3 ** -0.5, 3.5, ((2, 4),), jnp.float32)
    skip_gain = gaussian(arg_keys[4], (D,), 1.0, 6.0, ((0, 4),), jnp.float32)
    long_filter = gaussian(arg_keys[5], (GROUPS, SEQ), SEQ ** -0.5, 0.0234375, ((0, 4), (1, 8)), jnp.float32)
    return {"query_proj": query_proj, "key_proj": key_proj, "value_proj": value_proj, "short_taps": short_taps, "skip_gain": skip_gain, "long_filter": long_filter}


def depthwise(signal, taps):
    padded = jnp.pad(signal.astype(jnp.float32), ((2, 0), (0, 0)))
    return taps[0] * padded[2:] + taps[1] * padded[1:-1] + taps[2] * padded[:-2]


def reference(query_proj, key_proj, value_proj, short_taps, skip_gain, long_filter):
    results = []
    for group_idx in range(GROUPS):
        low_col = group_idx * GROUP_W
        high_col = low_col + GROUP_W
        query_short = depthwise(query_proj[:, low_col:high_col], short_taps[:, 0, low_col:high_col])
        key_short = depthwise(key_proj[:, low_col:high_col], short_taps[:, 1, low_col:high_col])
        value_short = depthwise(value_proj[:, low_col:high_col], short_taps[:, 2, low_col:high_col])
        gated = key_short * value_short
        spectrum = jnp.fft.rfft(gated, axis=0) * jnp.fft.rfft(long_filter[group_idx])[:, None]
        convolved = jnp.fft.irfft(spectrum, n=SEQ, axis=0)
        results.append(query_short * (convolved + skip_gain[low_col:high_col] * gated))
    return jnp.concatenate(results, axis=1)
```

```python
from functools import partial

import jax
import jax.numpy as jnp
import numpy as np
from jax import lax
from jax.experimental import pallas as pl
from jax.experimental.pallas import tpu as pltpu
from jax.sharding import PartitionSpec as P

A = 256
B = 256
LANES = 128

POWER = 15
TOP = 2.0**8.375
LEAST = 1e-34


def tables():
    index = np.arange(A)
    angle = 2.0 * np.pi / A * (np.outer(index, index) % A)
    cos, sin = np.cos(angle), -np.sin(angle)
    bf16 = jnp.bfloat16
    cos_hi, sin_hi = cos.astype(bf16), sin.astype(bf16)
    cos_lo = (cos - cos_hi.astype(np.float64)).astype(bf16)
    sin_lo = (sin - sin_hi.astype(np.float64)).astype(bf16)
    turn = 2.0 * np.pi / (A * B) * (np.outer(index, index) % (A * B))
    return cos_hi, sin_hi, cos_lo, sin_lo, np.cos(turn).astype(np.float32), np.sin(turn).astype(np.float32)


def matrices():
    cos_hi, sin_hi, cos_lo, sin_lo, turn_re, turn_im = (jnp.asarray(t) for t in tables())

    def real_form(re, im):
        return jnp.concatenate([jnp.concatenate([re, -im], axis=1), jnp.concatenate([im, re], axis=1)], axis=0)

    high, low = real_form(cos_hi, sin_hi), real_form(cos_lo, sin_lo)
    left = jnp.concatenate([high, low, high], axis=1)
    return left, left.T, turn_re, turn_im


def encode(scaled):
    cube = scaled * scaled * scaled
    sixth = cube * cube
    return sixth * sixth * cube


def decode(coded):
    size = jnp.exp2(jnp.log2(jnp.abs(coded)) * (1.0 / POWER))
    return jnp.where(coded < 0, -size, size)


def split(value):
    high = value.astype(jnp.bfloat16)
    return high, (value - high.astype(jnp.float32)).astype(jnp.bfloat16)


def left_dft(left, re, im):
    re_hi, re_lo = split(re)
    im_hi, im_lo = split(im)
    pieces = jnp.concatenate([re_hi, im_hi, re_hi, im_hi, re_lo, im_lo], axis=0)
    out = jnp.dot(left, pieces, preferred_element_type=jnp.float32)
    return out[:A], out[A:]


def right_dft(right, re, im):
    re_hi, re_lo = split(re)
    im_hi, im_lo = split(im)
    pieces = jnp.concatenate([re_hi, im_hi, re_hi, im_hi, re_lo, im_lo], axis=1)
    out = jnp.dot(pieces, right, preferred_element_type=jnp.float32)
    return out[:, :B], out[:, B:]


def short_conv(rows, before, taps, column):
    count = rows.shape[0]
    joined = jnp.concatenate([before, rows], axis=0)
    return (
        taps[0, column][None, :] * rows
        + taps[1, column][None, :] * joined[7 : 7 + count]
        + taps[2, column][None, :] * joined[6 : 6 + count]
    )


def pre_kernel(key_ref, value_ref, halo_ref, taps_ref, coded_ref, scale_ref, gated_ref):
    slabs = key_ref.shape[0] // B
    taps = taps_ref[...]

    def gate(slab, carry):
        key_before, value_before, most = carry
        rows = pl.ds(pl.multiple_of(slab * B, B), B)
        key = key_ref[rows, :].astype(jnp.float32)
        value = value_ref[rows, :].astype(jnp.float32)
        gated = short_conv(key, key_before, taps, 1) * short_conv(value, value_before, taps, 2)
        gated_ref[rows, :] = gated
        most = jnp.maximum(most, jnp.max(jnp.abs(gated).reshape(B // 8, 8, LANES), axis=0))
        return key[B - 8 :], value[B - 8 :], most

    start = (halo_ref[1].astype(jnp.float32), halo_ref[2].astype(jnp.float32), jnp.zeros((8, LANES), jnp.float32))
    _, _, most = lax.fori_loop(0, slabs, gate, start)
    most = jnp.maximum(jnp.max(most, axis=0, keepdims=True), LEAST)
    scale_ref[...] = most * (1.0 / TOP)
    factor = TOP / most

    def send(slab, _):
        rows = pl.ds(pl.multiple_of(slab * B, B), B)
        coded = encode(gated_ref[rows, :] * factor).T.astype(jnp.bfloat16)
        if len(coded_ref.shape) == 3:
            coded_ref[slab] = coded
        else:
            per = coded_ref.shape[2]
            for target in range(coded_ref.shape[0]):
                coded_ref[target, slab] = coded[target * per : (target + 1) * per]
        return 0

    lax.fori_loop(0, slabs, send, 0)


def spectrum_kernel(filter_ref, left_ref, right_ref, turn_re_ref, turn_im_ref, re_ref, im_ref):
    taps = filter_ref[...]
    re, im = left_dft(left_ref[...], taps, jnp.zeros_like(taps))
    cos, sin = turn_re_ref[...], turn_im_ref[...]
    re, im = right_dft(right_ref[...], re * cos + im * sin, im * cos - re * sin)
    re_ref[...] = re * (1.0 / (A * B))
    im_ref[...] = im * (1.0 / (A * B))


def conv_kernel(
    coded_ref, scale_ref, left_ref, right_ref, turn_re_ref, turn_im_ref, spec_re_ref, spec_im_ref,
    out_ref, out_scale_ref, work_ref,
):
    per = scale_ref.shape[1]

    def receive(slab, _):
        rows = pl.ds(pl.multiple_of(slab * A, A), A)
        value = decode(coded_ref[rows, :].astype(jnp.float32))
        for half in range(2):
            work_ref[half, rows, :] = value[:, half * LANES : (half + 1) * LANES]
        return 0

    lax.fori_loop(0, per, receive, 0)
    lane = lax.broadcasted_iota(jnp.int32, (A, per), 1)

    def signal(channel):
        scale = jnp.sum(jnp.where(lane == channel, scale_ref[...], 0.0), axis=1, keepdims=True)
        rows = pl.ds(channel, A, stride=per)
        return jnp.concatenate([work_ref[half, rows, :] for half in range(2)], axis=1) * scale

    def emit(channel, value):
        most = jnp.maximum(jnp.max(jnp.abs(value), keepdims=True), LEAST)
        out_scale_ref[pl.ds(channel, 1), :] = jnp.broadcast_to(most * (1.0 / TOP), (1, LANES))
        coded = encode(value * (TOP / most))
        for half in range(2):
            work_ref[half, pl.ds(channel, A, stride=per), :] = coded[:, half * LANES : (half + 1) * LANES]

    def pair(index, _):
        first, second = 2 * index, 2 * index + 1
        re, im = left_dft(left_ref[...], signal(first), signal(second))
        cos, sin = turn_re_ref[...], turn_im_ref[...]
        re, im = right_dft(right_ref[...], re * cos + im * sin, im * cos - re * sin)
        spec_re, spec_im = spec_re_ref[...], spec_im_ref[...]
        re, im = right_dft(right_ref[...], re * spec_re - im * spec_im, -(re * spec_im + im * spec_re))
        cos, sin = turn_re_ref[...], turn_im_ref[...]
        re, im = left_dft(left_ref[...], re * cos + im * sin, im * cos - re * sin)
        emit(first, re)
        emit(second, -im)
        return 0

    lax.fori_loop(0, per // 2, pair, 0)

    def send(slab, _):
        rows = pl.ds(pl.multiple_of(slab * A, A), A)
        out_ref[rows, :] = jnp.concatenate([work_ref[half, rows, :] for half in range(2)], axis=1).astype(jnp.bfloat16)
        return 0

    lax.fori_loop(0, per, send, 0)


def post_kernel(
    query_ref, key_ref, value_ref, halo_ref, taps_ref, skip_ref, coded_ref, scale_ref, *rest,
):
    out_ref, before_ref = rest[-2:]
    taps = taps_ref[...]
    slabs = query_ref.shape[0] // B

    @pl.when(pl.program_id(0) == 0)
    def _():
        before_ref[...] = halo_ref[...].astype(jnp.float32)

    def mix(slab, carry):
        query_before, key_before, value_before = carry
        rows = pl.ds(pl.multiple_of(slab * B, B), B)
        query = query_ref[rows, :].astype(jnp.float32)
        key = key_ref[rows, :].astype(jnp.float32)
        value = value_ref[rows, :].astype(jnp.float32)
        gated = short_conv(key, key_before, taps, 1) * short_conv(value, value_before, taps, 2)
        if len(coded_ref.shape) == 3:
            coded = coded_ref[slab]
        else:
            coded = jnp.concatenate([coded_ref[source, slab] for source in range(coded_ref.shape[0])], axis=0)
        convolved = decode(coded.astype(jnp.float32).T) * scale_ref[...]
        out_ref[rows, :] = short_conv(query, query_before, taps, 0) * (convolved + skip_ref[...] * gated)
        return query[B - 8 :], key[B - 8 :], value[B - 8 :]

    carry = lax.fori_loop(0, slabs, mix, (before_ref[0], before_ref[1], before_ref[2]))
    for which in range(3):
        before_ref[which] = carry[which]


def params():
    return pltpu.CompilerParams(vmem_limit_bytes=48 * 1024 * 1024)


def cost(flops, size):
    return pl.CostEstimate(flops=flops, bytes_accessed=size, transcendentals=0)


def per_device(query_proj, key_proj, value_proj, short_taps, skip_gain, long_filter):
    tok_count, chan_width = query_proj.shape
    seq_count = lax.axis_size("seq")
    slabs = tok_count // B
    chunks = chan_width // LANES
    per = LANES // seq_count
    aligned = per % 8 == 0

    ends = jnp.stack([query_proj[-8:], key_proj[-8:], value_proj[-8:]])
    halo = lax.ppermute(ends, "seq", [(source, source + 1) for source in range(seq_count - 1)])
    whole_filter = lax.all_gather(long_filter.reshape(slabs, B), "seq", axis=0, tiled=True)
    left, right, turn_re, turn_im = matrices()
    skip_row = skip_gain[None, :]

    coded_shape = (seq_count, slabs, per, B) if aligned else (slabs, LANES, B)
    swap = partial(lax.all_to_all, axis_name="seq", split_axis=0, concat_axis=0, tiled=True)

    def pre(chunk):
        coded, scale = pl.pallas_call(
            pre_kernel,
            grid=(1,),
            in_specs=[
                pl.BlockSpec((tok_count, LANES), lambda i: (0, chunk)),
                pl.BlockSpec((tok_count, LANES), lambda i: (0, chunk)),
                pl.BlockSpec((3, 8, LANES), lambda i: (0, 0, chunk)),
                pl.BlockSpec((3, 3, LANES), lambda i: (0, 0, chunk)),
            ],
            out_specs=[
                pl.BlockSpec(coded_shape, lambda i: (0,) * len(coded_shape)),
                pl.BlockSpec((1, LANES), lambda i: (0, 0)),
            ],
            out_shape=[
                jax.ShapeDtypeStruct(coded_shape, jnp.bfloat16),
                jax.ShapeDtypeStruct((1, LANES), jnp.float32),
            ],
            scratch_shapes=[pltpu.VMEM((tok_count, LANES), jnp.float32)],
            compiler_params=params(),
            cost_estimate=cost(40 * tok_count * LANES, 6 * tok_count * LANES),
            name="pre",
        )(key_proj, value_proj, halo, short_taps)
        if not aligned:
            coded = coded.reshape(slabs, seq_count, per, B).transpose(1, 0, 2, 3)
        return coded, scale.reshape(seq_count, per)

    def conv(coded, scale, spec_re, spec_im):
        rows = A * per
        return pl.pallas_call(
            conv_kernel,
            out_shape=[
                jax.ShapeDtypeStruct((rows, B), jnp.bfloat16),
                jax.ShapeDtypeStruct((per, LANES), jnp.float32),
            ],
            scratch_shapes=[pltpu.VMEM((2, rows, LANES), jnp.float32)],
            compiler_params=params(),
            cost_estimate=cost(per // 2 * 4 * 2 * 512 * 1536 * 256, 4 * rows * B),
            name="conv",
        )(coded.reshape(rows, B), jnp.repeat(scale, slabs, axis=0), left, right, turn_re, turn_im, spec_re, spec_im)

    def post(chunk, coded, scale, out):
        if not aligned:
            coded = coded.transpose(1, 0, 2, 3).reshape(slabs, LANES, B)
        step = min(1024, tok_count)
        block = step // B
        rows = pl.BlockSpec((step, LANES), lambda i: (i, chunk))
        coded_spec = (
            pl.BlockSpec((seq_count, block, per, B), lambda i: (0, i, 0, 0))
            if aligned
            else pl.BlockSpec((block, LANES, B), lambda i: (i, 0, 0))
        )
        in_specs = [
            rows,
            rows,
            rows,
            pl.BlockSpec((3, 8, LANES), lambda i: (0, 0, chunk)),
            pl.BlockSpec((3, 3, LANES), lambda i: (0, 0, chunk)),
            pl.BlockSpec((1, LANES), lambda i: (0, chunk)),
            coded_spec,
            pl.BlockSpec((1, LANES), lambda i: (0, 0)),
        ]
        args = [query_proj, key_proj, value_proj, halo, short_taps, skip_row, coded, scale]
        if out is not None:
            in_specs.append(pl.BlockSpec(memory_space=pl.ANY))
            args.append(out)
        return pl.pallas_call(
            post_kernel,
            grid=(tok_count // step,),
            in_specs=in_specs,
            out_specs=rows,
            out_shape=jax.ShapeDtypeStruct((tok_count, chan_width), jnp.float32),
            scratch_shapes=[pltpu.VMEM((3, 8, LANES), jnp.float32)],
            input_output_aliases={} if out is None else {len(args) - 1: 0},
            compiler_params=params(),
            cost_estimate=cost(60 * tok_count * LANES, 12 * tok_count * LANES),
            name="post",
        )(*args)

    spec_re, spec_im = pl.pallas_call(
        spectrum_kernel,
        out_shape=[jax.ShapeDtypeStruct((A, B), jnp.float32)] * 2,
        compiler_params=params(),
        cost_estimate=cost(2 * 2 * 512 * 1536 * 256, 4 * A * B),
        name="spectrum",
    )(whole_filter, left, right, turn_re, turn_im)

    received = []
    for chunk in range(chunks):
        coded, scale = pre(chunk)
        received.append((swap(coded), swap(scale)))
    returned = []
    for coded, scale in received:
        coded, scale = conv(coded, scale, spec_re, spec_im)
        coded = swap(coded.reshape(seq_count, slabs, per, B))
        scale = lax.all_gather(scale[:, 0], "seq", axis=0, tiled=True)
        returned.append((coded, scale.reshape(1, LANES)))
    out = None
    for chunk, (coded, scale) in enumerate(returned):
        out = post(chunk, coded, scale, out)
    return out


def solution(mesh):
    return jax.shard_map(
        per_device,
        mesh=mesh,
        in_specs=(
            P("seq", "chan"),
            P("seq", "chan"),
            P("seq", "chan"),
            P(None, None, "chan"),
            P("chan"),
            P("chan", "seq"),
        ),
        out_specs=P("seq", "chan"),
        check_vma=False,
    )
```

```python
from functools import partial

import jax
import jax.numpy as jnp
import numpy as np
from jax import lax
from jax.experimental import pallas as pl
from jax.experimental.pallas import tpu as pltpu
from jax.sharding import PartitionSpec as P

A = 256
B = 256
LANES = 128
EXTRA = 8

POWER = 15
TOP = 2.0**8.375
LEAST = 1e-34


def tables():
    index = np.arange(A)
    angle = 2.0 * np.pi / A * (np.outer(index, index) % A)
    cos, sin = np.cos(angle), -np.sin(angle)
    bf16 = jnp.bfloat16
    cos_hi, sin_hi = cos.astype(bf16), sin.astype(bf16)
    cos_lo = (cos - cos_hi.astype(np.float64)).astype(bf16)
    sin_lo = (sin - sin_hi.astype(np.float64)).astype(bf16)
    turn = 2.0 * np.pi / (A * B) * (np.outer(index, index) % (A * B))
    return cos_hi, sin_hi, cos_lo, sin_lo, np.cos(turn).astype(np.float32), np.sin(turn).astype(np.float32)


def encode(scaled):
    cube = scaled * scaled * scaled
    sixth = cube * cube
    return sixth * sixth * cube


def decode(coded):
    size = jnp.exp2(jnp.log2(jnp.abs(coded)) * (1.0 / POWER))
    return jnp.where(coded < 0, -size, size)


def split(value):
    high = value.astype(jnp.bfloat16)
    return high, (value - high.astype(jnp.float32)).astype(jnp.bfloat16)


def left_dft(left, pairs):
    high, low = split(jnp.concatenate([part for pair in pairs for part in pair], axis=1))
    out = jnp.dot(left, jnp.concatenate([high, high, low], axis=0), preferred_element_type=jnp.float32)
    result = []
    for index in range(len(pairs)):
        re, im = (out[:, (2 * index + part) * B : (2 * index + part + 1) * B] for part in range(2))
        result.append((re[:A] - im[A:], im[:A] + re[A:]))
    return result


def right_dft(right, pairs):
    pieces = []
    for re, im in pairs:
        re_hi, re_lo = split(re)
        im_hi, im_lo = split(im)
        pieces.append(jnp.concatenate([re_hi, im_hi, re_hi, im_hi, re_lo, im_lo], axis=1))
    out = jnp.dot(jnp.concatenate(pieces, axis=0), right, preferred_element_type=jnp.float32)
    return [(out[index * A : (index + 1) * A, :B], out[index * A : (index + 1) * A, B:]) for index in range(len(pairs))]


def turn(pairs, turn_re_ref, turn_im_ref):
    cos, sin = turn_re_ref[...], turn_im_ref[...]
    return [(re * cos + im * sin, im * cos - re * sin) for re, im in pairs]


def short_conv(rows, before, taps, column):
    count = rows.shape[0]
    joined = jnp.concatenate([before, rows], axis=0)
    return (
        taps[0, column][None, :] * rows
        + taps[1, column][None, :] * joined[7 : 7 + count]
        + taps[2, column][None, :] * joined[6 : 6 + count]
    )


def gate_all(key_ref, value_ref, halo_ref, taps_ref, gated_ref):
    taps = taps_ref[...]

    def gate(slab, carry):
        key_before, value_before, most = carry
        rows = pl.ds(pl.multiple_of(slab * B, B), B)
        key = key_ref[rows, :].astype(jnp.float32)
        value = value_ref[rows, :].astype(jnp.float32)
        gated = short_conv(key, key_before, taps, 1) * short_conv(value, value_before, taps, 2)
        gated_ref[rows, :] = gated
        most = jnp.maximum(most, jnp.max(jnp.abs(gated).reshape(B // 8, 8, LANES), axis=0))
        return key[B - 8 :], value[B - 8 :], most

    start = (halo_ref[1].astype(jnp.float32), halo_ref[2].astype(jnp.float32), jnp.zeros((8, LANES), jnp.float32))
    _, _, most = lax.fori_loop(0, key_ref.shape[0] // B, gate, start)
    return scale_of(jnp.max(most, axis=0, keepdims=True))


def scale_of(most):
    return (jnp.maximum(most, LEAST) * (1.0 / TOP)).astype(jnp.bfloat16).astype(jnp.float32)


def scale_tile(scale):
    return jnp.broadcast_to(jnp.concatenate([scale, scale], axis=1), (EXTRA, B)).astype(jnp.bfloat16)


def pre_whole_kernel(key_ref, value_ref, halo_ref, taps_ref, coded_ref, scale_ref, gated_ref):
    scale = gate_all(key_ref, value_ref, halo_ref, taps_ref, gated_ref)
    scale_ref[...] = scale
    factor = 1.0 / scale

    def send(slab, _):
        rows = pl.ds(pl.multiple_of(slab * B, B), B)
        coded_ref[slab] = encode(gated_ref[rows, :] * factor).T.astype(jnp.bfloat16)
        return 0

    lax.fori_loop(0, coded_ref.shape[0], send, 0)


def pre_parts_kernel(per, key_ref, value_ref, halo_ref, taps_ref, *rest):
    filter_refs, (parts_ref, gated_ref) = rest[:-2], rest[-2:]
    count, _, size, _ = parts_ref.shape
    slabs = key_ref.shape[0] // B
    scale = gate_all(key_ref, value_ref, halo_ref, taps_ref, gated_ref)
    factor = 1.0 / scale

    def send(slab, _):
        rows = pl.ds(pl.multiple_of(slab * B, B), B)
        coded = encode(gated_ref[rows, :] * factor).T.astype(jnp.bfloat16)
        place = pl.ds(pl.multiple_of(slab * per, per), per)
        for target in range(count):
            parts_ref[target, 0, place, :] = coded[target * per : (target + 1) * per]
        return 0

    lax.fori_loop(0, slabs, send, 0)
    tile = scale_tile(scale)
    for target in range(count):
        for filter_ref in filter_refs:
            parts_ref[target, 0, slabs * per : size - EXTRA, :] = jnp.concatenate(split(filter_ref[...]), axis=0)
        parts_ref[target, 0, size - EXTRA :, :] = tile


def parts_spectrum_kernel(parts_ref, *refs):
    *refs, filter_ref = refs
    slabs = parts_ref.shape[2] // 2
    for source in range(parts_ref.shape[0]):
        both = parts_ref[source, 0].astype(jnp.float32)
        filter_ref[source * slabs : (source + 1) * slabs, :] = both[:slabs] + both[slabs:]
    spectrum_kernel(filter_ref, *refs)


def spectrum_kernel(filter_ref, *refs):
    cos_hi, sin_hi, cos_lo, sin_lo = (ref[...] for ref in refs[:4])
    turn_re_ref, turn_im_ref, re_ref, im_ref, left_ref, right_ref = refs[4:]
    for piece, (cos, sin) in enumerate(((cos_hi, sin_hi), (cos_lo, sin_lo), (cos_hi, sin_hi))):
        left_ref[:A, piece * A : (piece + 1) * A] = cos
        left_ref[A:, piece * A : (piece + 1) * A] = sin
        right_ref[2 * piece * B : (2 * piece + 1) * B, :B] = cos
        right_ref[2 * piece * B : (2 * piece + 1) * B, B:] = sin
        right_ref[(2 * piece + 1) * B : (2 * piece + 2) * B, :B] = -sin
        right_ref[(2 * piece + 1) * B : (2 * piece + 2) * B, B:] = cos
    taps = filter_ref[...]
    pairs = left_dft(left_ref[...], [(taps, jnp.zeros_like(taps))])
    ((re, im),) = right_dft(right_ref[...], turn(pairs, turn_re_ref, turn_im_ref))
    re_ref[...] = re * (1.0 / (A * B))
    im_ref[...] = im * (1.0 / (A * B))


def put(work_ref, rows, value):
    for part in range(2):
        work_ref[part, rows, :] = value[:, part * LANES : (part + 1) * LANES]


def take(work_ref, rows):
    return jnp.concatenate([work_ref[part, rows, :] for part in range(2)], axis=1)


def convolve_all(per, base, scale_ref, left_ref, right_ref, turn_re_ref, turn_im_ref, spec_re_ref, spec_im_ref, work_ref):
    lane = lax.broadcasted_iota(jnp.int32, (A, LANES), 1)
    row_lane = lax.broadcasted_iota(jnp.int32, (1, LANES), 1)

    def signal(channel):
        scale = jnp.sum(jnp.where(lane == base + channel, scale_ref[...], 0.0), axis=1, keepdims=True)
        return take(work_ref, pl.ds(channel, A, stride=per)) * scale

    def emit(channel, value, scales):
        scale = scale_of(jnp.max(jnp.abs(value), keepdims=True))
        put(work_ref, pl.ds(channel, A, stride=per), encode(value * (1.0 / scale)))
        return jnp.where(row_lane == base + channel, scale, scales)

    together = 2 if per % 4 == 0 else 1

    def convolve(index, scales):
        first = 2 * together * index
        pairs = [(signal(first + 2 * which), signal(first + 2 * which + 1)) for which in range(together)]
        pairs = turn(left_dft(left_ref[...], pairs), turn_re_ref, turn_im_ref)
        pairs = right_dft(right_ref[...], pairs)
        spec_re, spec_im = spec_re_ref[...], spec_im_ref[...]
        pairs = [(re * spec_re - im * spec_im, -(re * spec_im + im * spec_re)) for re, im in pairs]
        pairs = turn(right_dft(right_ref[...], pairs), turn_re_ref, turn_im_ref)
        pairs = left_dft(left_ref[...], pairs)
        for which, (re, im) in enumerate(pairs):
            scales = emit(first + 2 * which, re, scales)
            scales = emit(first + 2 * which + 1, -im, scales)
        return scales

    return lax.fori_loop(0, per // (2 * together), convolve, jnp.zeros((1, LANES), jnp.float32))


def conv_whole_kernel(coded_ref, scale_ref, *rest):
    constants, (out_ref, out_scale_ref, work_ref) = rest[:6], rest[6:]
    per = coded_ref.shape[0] // A

    def receive(slab, _):
        rows = pl.ds(pl.multiple_of(slab * A, A), A)
        put(work_ref, rows, decode(coded_ref[rows, :].astype(jnp.float32)))
        return 0

    lax.fori_loop(0, per, receive, 0)
    scales = convolve_all(per, 0, scale_ref, *constants, work_ref)
    out_scale_ref[...] = jnp.broadcast_to(scales, out_scale_ref.shape)

    def send(slab, _):
        rows = pl.ds(pl.multiple_of(slab * A, A), A)
        out_ref[rows, :] = take(work_ref, rows).astype(jnp.bfloat16)
        return 0

    lax.fori_loop(0, per, send, 0)


def conv_parts_kernel(per, place_ref, parts_ref, *rest):
    constants, (out_ref, work_ref, scale_ref) = rest[:6], rest[6:]
    count, _, size, _ = parts_ref.shape
    out_size = out_ref.shape[2]
    slabs = A // count
    block = slabs * per
    steps = block // A

    def receive(index, _):
        for step in range(steps):
            value = parts_ref[index, 0, step * A : (step + 1) * A, :].astype(jnp.float32)
            put(work_ref, pl.ds(pl.multiple_of(index * block + step * A, A), A), decode(value))
        row = parts_ref[index, 0, size - EXTRA :, :LANES].astype(jnp.float32)[:1]
        scale_ref[pl.ds(pl.multiple_of(index * slabs, slabs), slabs), :] = jnp.broadcast_to(row, (slabs, LANES))
        return 0

    lax.fori_loop(0, count, receive, 0)
    tile = scale_tile(convolve_all(per, place_ref[0] * per, scale_ref, *constants, work_ref))

    def send(index, _):
        for step in range(steps):
            value = take(work_ref, pl.ds(pl.multiple_of(index * block + step * A, A), A))
            out_ref[index, 0, step * A : (step + 1) * A, :] = value.astype(jnp.bfloat16)
        out_ref[index, 0, out_size - EXTRA :, :] = tile
        return 0

    lax.fori_loop(0, count, send, 0)


def mix_all(step, query_ref, key_ref, value_ref, halo_ref, taps_ref, skip_ref, convolved_of, out_ref, before_ref):
    taps = taps_ref[...]

    @pl.when(step == 0)
    def _():
        before_ref[...] = halo_ref[...].astype(jnp.float32)

    def mix(slab, carry):
        query_before, key_before, value_before = carry
        rows = pl.ds(pl.multiple_of(slab * B, B), B)
        query = query_ref[rows, :].astype(jnp.float32)
        key = key_ref[rows, :].astype(jnp.float32)
        value = value_ref[rows, :].astype(jnp.float32)
        gated = short_conv(key, key_before, taps, 1) * short_conv(value, value_before, taps, 2)
        out_ref[rows, :] = short_conv(query, query_before, taps, 0) * (convolved_of(slab) + skip_ref[...] * gated)
        return query[B - 8 :], key[B - 8 :], value[B - 8 :]

    carry = lax.fori_loop(0, query_ref.shape[0] // B, mix, (before_ref[0], before_ref[1], before_ref[2]))
    for which in range(3):
        before_ref[which] = carry[which]


def post_whole_kernel(*refs):
    inputs, (coded_ref, scale_ref), (out_ref, before_ref) = refs[:6], refs[6:8], refs[-2:]

    def convolved_of(slab):
        return decode(coded_ref[slab].astype(jnp.float32).T) * scale_ref[...]

    mix_all(pl.program_id(0), *inputs, convolved_of, out_ref, before_ref)


def post_parts_kernel(*refs):
    inputs, (parts_ref, ends_ref), (out_ref, before_ref) = refs[:6], refs[6:8], refs[-2:]
    count = parts_ref.shape[0]
    per = LANES // count
    scale = jnp.zeros((EXTRA, LANES), jnp.float32)
    for source in range(count):
        scale = scale + ends_ref[source, 0].astype(jnp.float32)[:, :LANES]
    scale = scale[:1]

    def convolved_of(slab):
        place = pl.ds(pl.multiple_of(slab * per, per), per)
        coded = jnp.concatenate([parts_ref[source, 0, place, :] for source in range(count)], axis=0)
        return decode(coded.astype(jnp.float32).T) * scale

    mix_all(pl.program_id(1), *inputs, convolved_of, out_ref, before_ref)


def params():
    return pltpu.CompilerParams(vmem_limit_bytes=48 * 1024 * 1024)


def cost(flops, size):
    return pl.CostEstimate(flops=flops // 1000, bytes_accessed=size // 1000, transcendentals=0)


SCALAR = pl.BlockSpec(memory_space=pltpu.SMEM)


def per_device(query_proj, key_proj, value_proj, short_taps, skip_gain, long_filter):
    tok_count, chan_width = query_proj.shape
    seq_count = lax.axis_size("seq")
    slabs = tok_count // B
    chunks = chan_width // LANES
    per = LANES // seq_count
    in_parts = per % 16 == 0 and (slabs * per) % A == 0 and slabs % 8 == 0 and seq_count & (seq_count - 1) == 0
    size = slabs * per + EXTRA
    place = lax.axis_index("seq").astype(jnp.int32).reshape(1)

    ends = jnp.stack([query_proj[-8:], key_proj[-8:], value_proj[-8:]])
    halo = lax.ppermute(ends, "seq", [(source, source + 1) for source in range(seq_count - 1)])
    skip_row = skip_gain[None, :]

    swap = partial(lax.all_to_all, axis_name="seq", split_axis=0, concat_axis=0, tiled=True)

    def whole_block(shape):
        return pl.BlockSpec(shape, lambda i: (0,) * len(shape))

    def pre(chunk, count, *filters):
        rows = pl.BlockSpec((tok_count, LANES), lambda i: (0, chunk + i))
        if in_parts:
            rows_out = size + 2 * slabs * len(filters)
            out_shape = [jax.ShapeDtypeStruct((seq_count, count, rows_out, B), jnp.bfloat16)]
            out_specs = [pl.BlockSpec((seq_count, 1, rows_out, B), lambda i: (0, i, 0, 0))]
        else:
            out_shape = [
                jax.ShapeDtypeStruct((slabs, LANES, B), jnp.bfloat16),
                jax.ShapeDtypeStruct((1, LANES), jnp.float32),
            ]
            out_specs = [whole_block(out.shape) for out in out_shape]
        return pl.pallas_call(
            partial(pre_parts_kernel, per) if in_parts else pre_whole_kernel,
            grid=(count,),
            in_specs=[
                rows,
                rows,
                pl.BlockSpec((3, 8, LANES), lambda i: (0, 0, chunk + i)),
                pl.BlockSpec((3, 3, LANES), lambda i: (0, 0, chunk + i)),
            ]
            + [whole_block((slabs, B))] * len(filters),
            out_specs=out_specs,
            out_shape=out_shape,
            scratch_shapes=[pltpu.VMEM((tok_count, LANES), jnp.float32)],
            compiler_params=params(),
            cost_estimate=cost(count * 40 * tok_count * LANES, count * 6 * tok_count * LANES),
            name="pre",
        )(key_proj, value_proj, halo, short_taps, *filters)

    def conv(first, count, coded, *scale):
        rows = A * per
        args = (coded, *scale, left, right, turn_re, turn_im, spec_re, spec_im)
        in_specs = [whole_block(arg.shape) for arg in args]
        scratch = [pltpu.VMEM((2, rows, LANES), jnp.float32)]
        if in_parts:
            args = (place,) + args
            block = (seq_count, 1, coded.shape[2], B)
            in_specs = [SCALAR, pl.BlockSpec(block, lambda i: (0, first + i, 0, 0))] + in_specs[1:]
            out_shape = [jax.ShapeDtypeStruct((seq_count, count, size, B), jnp.bfloat16)]
            out_specs = [pl.BlockSpec((seq_count, 1, size, B), lambda i: (0, i, 0, 0))]
            scratch.append(pltpu.VMEM((A, LANES), jnp.float32))
        else:
            out_shape = [
                jax.ShapeDtypeStruct((rows, B), jnp.bfloat16),
                jax.ShapeDtypeStruct((8, LANES), jnp.float32),
            ]
            out_specs = [whole_block(out.shape) for out in out_shape]
        return pl.pallas_call(
            partial(conv_parts_kernel, per) if in_parts else conv_whole_kernel,
            grid=(count,),
            in_specs=in_specs,
            out_specs=out_specs,
            out_shape=out_shape,
            scratch_shapes=scratch,
            compiler_params=params(),
            cost_estimate=cost(count * per // 2 * 4 * 2 * 512 * 1536 * 256, count * 4 * rows * B),
            name="conv",
        )(*args)

    def post(chunk, count, out, coded, *scale):
        step = min(1024, tok_count)
        block = step // B
        rows = pl.BlockSpec((step, LANES), lambda u, i: (i, chunk + u))
        in_specs = [
            rows,
            rows,
            rows,
            pl.BlockSpec((3, 8, LANES), lambda u, i: (0, 0, chunk + u)),
            pl.BlockSpec((3, 3, LANES), lambda u, i: (0, 0, chunk + u)),
            pl.BlockSpec((1, LANES), lambda u, i: (0, chunk + u)),
        ]
        args = [query_proj, key_proj, value_proj, halo, short_taps, skip_row]
        if in_parts:
            last = slabs * per // EXTRA
            in_specs += [
                pl.BlockSpec((seq_count, 1, block * per, B), lambda u, i: (0, u, i, 0)),
                pl.BlockSpec((seq_count, 1, EXTRA, B), lambda u, i: (0, u, last, 0)),
            ]
            args += [coded, coded]
        else:
            in_specs += [
                pl.BlockSpec((block, LANES, B), lambda u, i: (i, 0, 0)),
                pl.BlockSpec((1, LANES), lambda u, i: (0, 0)),
            ]
            args += [coded, *scale]
        if out is not None:
            in_specs.append(pl.BlockSpec(memory_space=pl.ANY))
            args.append(out)
        return pl.pallas_call(
            post_parts_kernel if in_parts else post_whole_kernel,
            grid=(count, tok_count // step),
            in_specs=in_specs,
            out_specs=rows,
            out_shape=jax.ShapeDtypeStruct((tok_count, chan_width), jnp.float32),
            scratch_shapes=[pltpu.VMEM((3, 8, LANES), jnp.float32)],
            input_output_aliases={} if out is None else {len(args) - 1: 0},
            compiler_params=params(),
            cost_estimate=cost(count * 60 * tok_count * LANES, count * 12 * tok_count * LANES),
            name="post",
        )(*args)

    own_filter = long_filter.reshape(slabs, B)
    if in_parts:
        arrived = [(0, swap(*pre(0, 1, own_filter)))]
        if chunks > 1:
            arrived.append((1, swap(*pre(1, chunks - 1))))
        whole_filter = arrived[0][1]
        filter_spec = pl.BlockSpec((seq_count, 1, 2 * slabs, B), lambda i: (0, 0, per // 2, 0))
    else:
        whole_filter = swap(jnp.broadcast_to(own_filter, (seq_count, slabs, B))).reshape(A, B)
        filter_spec = whole_block((A, B))
    cos_hi, sin_hi, cos_lo, sin_lo, turn_re, turn_im = (jnp.asarray(table) for table in tables())
    filter_args = (whole_filter, cos_hi, sin_hi, cos_lo, sin_lo, turn_re, turn_im)
    spec_shape = [jax.ShapeDtypeStruct((A, B), jnp.float32)] * 2
    spec_shape += [jax.ShapeDtypeStruct((2 * A, 3 * A), jnp.bfloat16), jax.ShapeDtypeStruct((6 * B, 2 * B), jnp.bfloat16)]
    spec_re, spec_im, left, right = pl.pallas_call(
        parts_spectrum_kernel if in_parts else spectrum_kernel,
        grid=(1,),
        in_specs=[filter_spec] + [whole_block((A, B))] * 6,
        out_specs=[whole_block(out.shape) for out in spec_shape],
        out_shape=spec_shape,
        scratch_shapes=[pltpu.VMEM((A, B), jnp.float32)] * in_parts,
        compiler_params=params(),
        cost_estimate=cost(2 * 2 * 512 * 1536 * 256, 16 * A * B),
        name="spectrum",
    )(*filter_args)

    out = None
    if in_parts:
        cuts = sorted({0, 1, chunks - 1, chunks})
        returned = []
        for start, stop in zip(cuts[:-1], cuts[1:]):
            source, coded = arrived[min(start, 1)]
            returned.append((start, stop - start, swap(*conv(start - source, stop - start, coded))))
        for start, count, coded in returned:
            out = post(start, count, out, coded)
    else:
        returned = []
        for chunk in range(chunks):
            coded, scale = pre(chunk, 1)
            coded = swap(coded.reshape(slabs, seq_count, per, B).transpose(1, 0, 2, 3))
            scale = jnp.repeat(swap(scale.reshape(seq_count, per)), slabs, axis=0)
            scale = jnp.pad(scale, ((0, 0), (0, LANES - per)))
            coded, scale = conv(0, 1, coded.reshape(A * per, B), scale)
            coded = swap(coded.reshape(seq_count, slabs, per, B))
            scale = lax.all_gather(scale[0, :per], "seq", axis=0, tiled=True)
            returned.append((coded.transpose(1, 0, 2, 3).reshape(slabs, LANES, B), scale.reshape(1, LANES)))
        for chunk, (coded, scale) in enumerate(returned):
            out = post(chunk, 1, out, coded, scale)
    return out


def solution(mesh):
    return jax.shard_map(
        per_device,
        mesh=mesh,
        in_specs=(
            P("seq", "chan"),
            P("seq", "chan"),
            P("seq", "chan"),
            P(None, None, "chan"),
            P("chan"),
            P("chan", "seq"),
        ),
        out_specs=P("seq", "chan"),
        check_vma=False,
    )
```

```python
from functools import partial

import jax
import jax.numpy as jnp
import numpy as np
from jax import lax
from jax.experimental import pallas as pl
from jax.experimental.pallas import tpu as pltpu
from jax.sharding import PartitionSpec as P

A = 256
B = 256
LANES = 128
EXTRA = 8

POWER = 15
TOP = 2.0**8.375
LEAST = 1e-34


def tables():
    index = np.arange(A)
    angle = 2.0 * np.pi / A * (np.outer(index, index) % A)
    cos, sin = np.cos(angle), -np.sin(angle)
    bf16 = jnp.bfloat16
    cos_hi, sin_hi = cos.astype(bf16), sin.astype(bf16)
    cos_lo = (cos - cos_hi.astype(np.float64)).astype(bf16)
    sin_lo = (sin - sin_hi.astype(np.float64)).astype(bf16)
    turn = 2.0 * np.pi / (A * B) * (np.outer(index, index) % (A * B))
    return cos_hi, sin_hi, cos_lo, sin_lo, np.cos(turn).astype(np.float32), np.sin(turn).astype(np.float32)


def encode(scaled):
    cube = scaled * scaled * scaled
    sixth = cube * cube
    return sixth * sixth * cube


def decode(coded):
    size = jnp.exp2(jnp.log2(jnp.abs(coded)) * (1.0 / POWER))
    return jnp.where(coded < 0, -size, size)


def split(value):
    high = value.astype(jnp.bfloat16)
    return high, (value - high.astype(jnp.float32)).astype(jnp.bfloat16)


def left_dft(left, pairs):
    high, low = split(jnp.concatenate([part for pair in pairs for part in pair], axis=1))
    out = jnp.dot(left, jnp.concatenate([high, high, low], axis=0), preferred_element_type=jnp.float32)
    result = []
    for index in range(len(pairs)):
        re, im = (out[:, (2 * index + part) * B : (2 * index + part + 1) * B] for part in range(2))
        result.append((re[:A] - im[A:], im[:A] + re[A:]))
    return result


def right_dft(right, pairs):
    pieces = []
    for re, im in pairs:
        re_hi, re_lo = split(re)
        im_hi, im_lo = split(im)
        pieces.append(jnp.concatenate([re_hi, im_hi, re_hi, im_hi, re_lo, im_lo], axis=1))
    out = jnp.dot(jnp.concatenate(pieces, axis=0), right, preferred_element_type=jnp.float32)
    return [(out[index * A : (index + 1) * A, :B], out[index * A : (index + 1) * A, B:]) for index in range(len(pairs))]


def turn(pairs, turn_re_ref, turn_im_ref):
    cos, sin = turn_re_ref[...], turn_im_ref[...]
    return [(re * cos + im * sin, im * cos - re * sin) for re, im in pairs]


def short_conv(window_ref, which, rows, taps, column):
    window_ref[which, :8, :] = window_ref[which, B:, :]
    window_ref[which, 8:, :] = rows
    return (
        taps[0, column][None, :] * rows
        + taps[1, column][None, :] * window_ref[which, 7 : 7 + B, :]
        + taps[2, column][None, :] * window_ref[which, 6 : 6 + B, :]
    )


def gate_all(key_ref, value_ref, halo_ref, taps_ref, gated_ref, window_ref):
    taps = taps_ref[...]
    for which in range(1, 3):
        window_ref[which, B:, :] = halo_ref[which].astype(jnp.float32)

    def gate(slab, most):
        rows = pl.ds(pl.multiple_of(slab * B, B), B)
        key = short_conv(window_ref, 1, key_ref[rows, :].astype(jnp.float32), taps, 1)
        value = short_conv(window_ref, 2, value_ref[rows, :].astype(jnp.float32), taps, 2)
        gated = key * value
        gated_ref[rows, :] = gated
        return jnp.maximum(most, jnp.max(jnp.abs(gated).reshape(B // 8, 8, LANES), axis=0))

    most = lax.fori_loop(0, key_ref.shape[0] // B, gate, jnp.zeros((8, LANES), jnp.float32))
    return scale_of(jnp.max(most, axis=0, keepdims=True))


def scale_of(most):
    return (jnp.maximum(most, LEAST) * (1.0 / TOP)).astype(jnp.bfloat16).astype(jnp.float32)


def scale_tile(scale):
    return jnp.broadcast_to(jnp.concatenate([scale, scale], axis=1), (EXTRA, B)).astype(jnp.bfloat16)


def pre_whole_kernel(key_ref, value_ref, halo_ref, taps_ref, coded_ref, scale_ref, gated_ref, window_ref):
    scale = gate_all(key_ref, value_ref, halo_ref, taps_ref, gated_ref, window_ref)
    scale_ref[...] = scale
    factor = 1.0 / scale

    def send(slab, _):
        rows = pl.ds(pl.multiple_of(slab * B, B), B)
        coded_ref[slab] = encode(gated_ref[rows, :] * factor).astype(jnp.bfloat16).T
        return 0

    lax.fori_loop(0, coded_ref.shape[0], send, 0)


def pre_parts_kernel(per, key_ref, value_ref, halo_ref, taps_ref, *rest):
    filter_refs, (parts_ref, gated_ref, window_ref) = rest[:-3], rest[-3:]
    count, _, size, _ = parts_ref.shape
    slabs = key_ref.shape[0] // B
    scale = gate_all(key_ref, value_ref, halo_ref, taps_ref, gated_ref, window_ref)
    factor = 1.0 / scale

    def send(slab, _):
        rows = pl.ds(pl.multiple_of(slab * B, B), B)
        coded = encode(gated_ref[rows, :] * factor).astype(jnp.bfloat16).T
        place = pl.ds(pl.multiple_of(slab * per, per), per)
        for target in range(count):
            parts_ref[target, 0, place, :] = coded[target * per : (target + 1) * per]
        return 0

    lax.fori_loop(0, slabs, send, 0)
    tile = scale_tile(scale)
    for target in range(count):
        for filter_ref in filter_refs:
            parts_ref[target, 0, slabs * per : size - EXTRA, :] = jnp.concatenate(split(filter_ref[...]), axis=0)
        parts_ref[target, 0, size - EXTRA :, :] = tile


def parts_spectrum_kernel(parts_ref, *refs):
    *refs, filter_ref = refs
    slabs = parts_ref.shape[2] // 2
    for source in range(parts_ref.shape[0]):
        both = parts_ref[source, 0].astype(jnp.float32)
        filter_ref[source * slabs : (source + 1) * slabs, :] = both[:slabs] + both[slabs:]
    spectrum_kernel(filter_ref, *refs)


def spectrum_kernel(filter_ref, *refs):
    cos_hi, sin_hi, cos_lo, sin_lo = (ref[...] for ref in refs[:4])
    turn_re_ref, turn_im_ref, re_ref, im_ref, left_ref, right_ref = refs[4:]
    for piece, (cos, sin) in enumerate(((cos_hi, sin_hi), (cos_lo, sin_lo), (cos_hi, sin_hi))):
        left_ref[:A, piece * A : (piece + 1) * A] = cos
        left_ref[A:, piece * A : (piece + 1) * A] = sin
        right_ref[2 * piece * B : (2 * piece + 1) * B, :B] = cos
        right_ref[2 * piece * B : (2 * piece + 1) * B, B:] = sin
        right_ref[(2 * piece + 1) * B : (2 * piece + 2) * B, :B] = -sin
        right_ref[(2 * piece + 1) * B : (2 * piece + 2) * B, B:] = cos
    taps = filter_ref[...]
    pairs = left_dft(left_ref[...], [(taps, jnp.zeros_like(taps))])
    ((re, im),) = right_dft(right_ref[...], turn(pairs, turn_re_ref, turn_im_ref))
    re_ref[...] = re * (1.0 / (A * B))
    im_ref[...] = im * (1.0 / (A * B))


def put(work_ref, rows, value):
    for part in range(2):
        work_ref[part, rows, :] = value[:, part * LANES : (part + 1) * LANES]


def take(work_ref, rows):
    return jnp.concatenate([work_ref[part, rows, :] for part in range(2)], axis=1)


def convolve_all(per, base, scale_ref, left_ref, right_ref, turn_re_ref, turn_im_ref, spec_re_ref, spec_im_ref, work_ref):
    lane = lax.broadcasted_iota(jnp.int32, (A, LANES), 1)
    row_lane = lax.broadcasted_iota(jnp.int32, (1, LANES), 1)

    def signal(channel):
        scale = jnp.sum(jnp.where(lane == base + channel, scale_ref[...], 0.0), axis=1, keepdims=True)
        return take(work_ref, pl.ds(channel, A, stride=per)) * scale

    def emit(channel, value, scales):
        scale = scale_of(jnp.max(jnp.abs(value), keepdims=True))
        put(work_ref, pl.ds(channel, A, stride=per), encode(value * (1.0 / scale)))
        return jnp.where(row_lane == base + channel, scale, scales)

    together = 2 if per % 4 == 0 else 1

    def convolve(index, scales):
        first = 2 * together * index
        pairs = [(signal(first + 2 * which), signal(first + 2 * which + 1)) for which in range(together)]
        pairs = turn(left_dft(left_ref[...], pairs), turn_re_ref, turn_im_ref)
        pairs = right_dft(right_ref[...], pairs)
        spec_re, spec_im = spec_re_ref[...], spec_im_ref[...]
        pairs = [(re * spec_re - im * spec_im, -(re * spec_im + im * spec_re)) for re, im in pairs]
        pairs = turn(right_dft(right_ref[...], pairs), turn_re_ref, turn_im_ref)
        pairs = left_dft(left_ref[...], pairs)
        for which, (re, im) in enumerate(pairs):
            scales = emit(first + 2 * which, re, scales)
            scales = emit(first + 2 * which + 1, -im, scales)
        return scales

    return lax.fori_loop(0, per // (2 * together), convolve, jnp.zeros((1, LANES), jnp.float32))


def conv_whole_kernel(coded_ref, scale_ref, *rest):
    constants, (out_ref, out_scale_ref, work_ref) = rest[:6], rest[6:]
    per = coded_ref.shape[0] // A

    def receive(slab, _):
        rows = pl.ds(pl.multiple_of(slab * A, A), A)
        put(work_ref, rows, decode(coded_ref[rows, :].astype(jnp.float32)))
        return 0

    lax.fori_loop(0, per, receive, 0)
    scales = convolve_all(per, 0, scale_ref, *constants, work_ref)
    out_scale_ref[...] = jnp.broadcast_to(scales, out_scale_ref.shape)

    def send(slab, _):
        rows = pl.ds(pl.multiple_of(slab * A, A), A)
        out_ref[rows, :] = take(work_ref, rows).astype(jnp.bfloat16)
        return 0

    lax.fori_loop(0, per, send, 0)


def conv_parts_kernel(per, place_ref, parts_ref, *rest):
    sources, (out_ref, work_ref, scale_ref), constants, sems = rest[:6], rest[6:9], rest[9:15], rest[15]
    copies = [pltpu.make_async_copy(*pair, sems.at[index]) for index, pair in enumerate(zip(sources, constants))]

    @pl.when(pl.program_id(0) == 0)
    def _():
        for copy in copies:
            copy.start()

    count, _, size, _ = parts_ref.shape
    out_size = out_ref.shape[2]
    slabs = A // count
    block = slabs * per
    steps = block // A

    def receive(index, _):
        for step in range(steps):
            value = parts_ref[index, 0, step * A : (step + 1) * A, :].astype(jnp.float32)
            put(work_ref, pl.ds(pl.multiple_of(index * block + step * A, A), A), decode(value))
        row = parts_ref[index, 0, size - EXTRA :, :LANES].astype(jnp.float32)[:1]
        scale_ref[pl.ds(pl.multiple_of(index * slabs, slabs), slabs), :] = jnp.broadcast_to(row, (slabs, LANES))
        return 0

    lax.fori_loop(0, count, receive, 0)

    @pl.when(pl.program_id(0) == 0)
    def _():
        for copy in copies:
            copy.wait()

    tile = scale_tile(convolve_all(per, place_ref[0] * per, scale_ref, *constants, work_ref))

    def send(index, _):
        for step in range(steps):
            value = take(work_ref, pl.ds(pl.multiple_of(index * block + step * A, A), A))
            out_ref[index, 0, step * A : (step + 1) * A, :] = value.astype(jnp.bfloat16)
        out_ref[index, 0, out_size - EXTRA :, :] = tile
        return 0

    lax.fori_loop(0, count, send, 0)


def mix_all(step, query_ref, key_ref, value_ref, halo_ref, taps_ref, skip_ref, convolved_of, out_ref, window_ref):
    taps = taps_ref[...]

    @pl.when(step == 0)
    def _():
        for which in range(3):
            window_ref[which, B:, :] = halo_ref[which].astype(jnp.float32)

    def mix(slab, _):
        rows = pl.ds(pl.multiple_of(slab * B, B), B)
        query, key, value = (
            short_conv(window_ref, which, ref[rows, :].astype(jnp.float32), taps, which)
            for which, ref in enumerate((query_ref, key_ref, value_ref))
        )
        out_ref[rows, :] = query * (convolved_of(slab) + skip_ref[...] * (key * value))
        return 0

    lax.fori_loop(0, query_ref.shape[0] // B, mix, 0)


def post_whole_kernel(*refs):
    inputs, (coded_ref, scale_ref), (out_ref, window_ref) = refs[:6], refs[6:8], refs[-2:]

    def convolved_of(slab):
        return decode(coded_ref[slab].T.astype(jnp.float32)) * scale_ref[...]

    mix_all(pl.program_id(0), *inputs, convolved_of, out_ref, window_ref)


def post_parts_kernel(*refs):
    inputs, (parts_ref, ends_ref), (out_ref, window_ref) = refs[:6], refs[6:8], refs[-2:]
    count = parts_ref.shape[0]
    per = LANES // count
    scale = jnp.zeros((EXTRA, LANES), jnp.float32)
    for source in range(count):
        scale = scale + ends_ref[source, 0].astype(jnp.float32)[:, :LANES]
    scale = scale[:1]

    def convolved_of(slab):
        place = pl.ds(pl.multiple_of(slab * per, per), per)
        coded = jnp.concatenate([parts_ref[source, 0, place, :] for source in range(count)], axis=0)
        return decode(coded.T.astype(jnp.float32)) * scale

    mix_all(pl.program_id(1), *inputs, convolved_of, out_ref, window_ref)


def params():
    return pltpu.CompilerParams(vmem_limit_bytes=48 * 1024 * 1024)


def cost(flops, size):
    return pl.CostEstimate(flops=flops // 1000, bytes_accessed=size // 1000, transcendentals=0)


SCALAR = pl.BlockSpec(memory_space=pltpu.SMEM)


def per_device(query_proj, key_proj, value_proj, short_taps, skip_gain, long_filter):
    tok_count, chan_width = query_proj.shape
    seq_count = lax.axis_size("seq")
    slabs = tok_count // B
    chunks = chan_width // LANES
    per = LANES // seq_count
    in_parts = per % 16 == 0 and (slabs * per) % A == 0 and slabs % 8 == 0 and seq_count & (seq_count - 1) == 0
    size = slabs * per + EXTRA
    place = lax.axis_index("seq").astype(jnp.int32).reshape(1)

    ends = jnp.stack([query_proj[-8:], key_proj[-8:], value_proj[-8:]])
    halo = lax.ppermute(ends, "seq", [(source, source + 1) for source in range(seq_count - 1)])
    skip_row = skip_gain[None, :]

    swap = partial(lax.all_to_all, axis_name="seq", split_axis=0, concat_axis=0, tiled=True)

    def whole_block(shape):
        return pl.BlockSpec(shape, lambda i: (0,) * len(shape))

    def pre(chunk, count, *filters):
        rows = pl.BlockSpec((tok_count, LANES), lambda i: (0, chunk + i))
        if in_parts:
            rows_out = size + 2 * slabs * len(filters)
            out_shape = [jax.ShapeDtypeStruct((seq_count, count, rows_out, B), jnp.bfloat16)]
            out_specs = [pl.BlockSpec((seq_count, 1, rows_out, B), lambda i: (0, i, 0, 0))]
        else:
            out_shape = [
                jax.ShapeDtypeStruct((slabs, LANES, B), jnp.bfloat16),
                jax.ShapeDtypeStruct((1, LANES), jnp.float32),
            ]
            out_specs = [whole_block(out.shape) for out in out_shape]
        return pl.pallas_call(
            partial(pre_parts_kernel, per) if in_parts else pre_whole_kernel,
            grid=(count,),
            in_specs=[
                rows,
                rows,
                pl.BlockSpec((3, 8, LANES), lambda i: (0, 0, chunk + i)),
                pl.BlockSpec((3, 3, LANES), lambda i: (0, 0, chunk + i)),
            ]
            + [whole_block((slabs, B))] * len(filters),
            out_specs=out_specs,
            out_shape=out_shape,
            scratch_shapes=[pltpu.VMEM((tok_count, LANES), jnp.float32), pltpu.VMEM((3, 8 + B, LANES), jnp.float32)],
            compiler_params=params(),
            cost_estimate=cost(count * 40 * tok_count * LANES, count * 6 * tok_count * LANES),
            name="pre",
        )(key_proj, value_proj, halo, short_taps, *filters)

    def conv(first, count, coded, *scale):
        rows = A * per
        args = (coded, *scale, left, right, turn_re, turn_im, spec_re, spec_im)
        in_specs = [whole_block(arg.shape) for arg in args]
        scratch = [pltpu.VMEM((2, rows, LANES), jnp.float32)]
        if in_parts:
            args = (place,) + args
            block = (seq_count, 1, coded.shape[2], B)
            in_specs = [SCALAR, pl.BlockSpec(block, lambda i: (0, first + i, 0, 0))]
            in_specs += [pl.BlockSpec(memory_space=pltpu.HBM)] * 6
            out_shape = [jax.ShapeDtypeStruct((seq_count, count, size, B), jnp.bfloat16)]
            out_specs = [pl.BlockSpec((seq_count, 1, size, B), lambda i: (0, i, 0, 0))]
            scratch.append(pltpu.VMEM((A, LANES), jnp.float32))
            scratch += [pltpu.VMEM(arg.shape, arg.dtype) for arg in args[2:]] + [pltpu.SemaphoreType.DMA((6,))]
        else:
            out_shape = [
                jax.ShapeDtypeStruct((rows, B), jnp.bfloat16),
                jax.ShapeDtypeStruct((8, LANES), jnp.float32),
            ]
            out_specs = [whole_block(out.shape) for out in out_shape]
        return pl.pallas_call(
            partial(conv_parts_kernel, per) if in_parts else conv_whole_kernel,
            grid=(count,),
            in_specs=in_specs,
            out_specs=out_specs,
            out_shape=out_shape,
            scratch_shapes=scratch,
            compiler_params=params(),
            cost_estimate=cost(count * per // 2 * 4 * 2 * 512 * 1536 * 256, count * 4 * rows * B),
            name="conv",
        )(*args)

    def post(chunk, count, out, coded, *scale):
        step = min(2048, tok_count)
        block = step // B
        rows = pl.BlockSpec((step, LANES), lambda u, i: (i, chunk + u))
        in_specs = [
            rows,
            rows,
            rows,
            pl.BlockSpec((3, 8, LANES), lambda u, i: (0, 0, chunk + u)),
            pl.BlockSpec((3, 3, LANES), lambda u, i: (0, 0, chunk + u)),
            pl.BlockSpec((1, LANES), lambda u, i: (0, chunk + u)),
        ]
        args = [query_proj, key_proj, value_proj, halo, short_taps, skip_row]
        if in_parts:
            last = slabs * per // EXTRA
            in_specs += [
                pl.BlockSpec((seq_count, 1, block * per, B), lambda u, i: (0, u, i, 0)),
                pl.BlockSpec((seq_count, 1, EXTRA, B), lambda u, i: (0, u, last, 0)),
            ]
            args += [coded, coded]
        else:
            in_specs += [
                pl.BlockSpec((block, LANES, B), lambda u, i: (i, 0, 0)),
                pl.BlockSpec((1, LANES), lambda u, i: (0, 0)),
            ]
            args += [coded, *scale]
        if out is not None:
            in_specs.append(pl.BlockSpec(memory_space=pl.ANY))
            args.append(out)
        return pl.pallas_call(
            post_parts_kernel if in_parts else post_whole_kernel,
            grid=(count, tok_count // step),
            in_specs=in_specs,
            out_specs=rows,
            out_shape=jax.ShapeDtypeStruct((tok_count, chan_width), jnp.float32),
            scratch_shapes=[pltpu.VMEM((3, 8 + B, LANES), jnp.float32)],
            input_output_aliases={} if out is None else {len(args) - 1: 0},
            compiler_params=params(),
            cost_estimate=cost(count * 60 * tok_count * LANES, count * 12 * tok_count * LANES),
            name="post",
        )(*args)

    own_filter = long_filter.reshape(slabs, B)
    if in_parts:
        arrived = [(0, swap(*pre(0, 1, own_filter)))]
        if chunks > 1:
            arrived.append((1, swap(*pre(1, chunks - 1))))
        whole_filter = arrived[0][1]
        filter_spec = pl.BlockSpec((seq_count, 1, 2 * slabs, B), lambda i: (0, 0, per // 2, 0))
    else:
        whole_filter = swap(jnp.broadcast_to(own_filter, (seq_count, slabs, B))).reshape(A, B)
        filter_spec = whole_block((A, B))
    cos_hi, sin_hi, cos_lo, sin_lo, turn_re, turn_im = (jnp.asarray(table) for table in tables())
    filter_args = (whole_filter, cos_hi, sin_hi, cos_lo, sin_lo, turn_re, turn_im)
    spec_shape = [jax.ShapeDtypeStruct((A, B), jnp.float32)] * 2
    spec_shape += [jax.ShapeDtypeStruct((2 * A, 3 * A), jnp.bfloat16), jax.ShapeDtypeStruct((6 * B, 2 * B), jnp.bfloat16)]
    spec_re, spec_im, left, right = pl.pallas_call(
        parts_spectrum_kernel if in_parts else spectrum_kernel,
        grid=(1,),
        in_specs=[filter_spec] + [whole_block((A, B))] * 6,
        out_specs=[whole_block(out.shape) for out in spec_shape],
        out_shape=spec_shape,
        scratch_shapes=[pltpu.VMEM((A, B), jnp.float32)] * in_parts,
        compiler_params=params(),
        cost_estimate=cost(2 * 2 * 512 * 1536 * 256, 16 * A * B),
        name="spectrum",
    )(*filter_args)

    out = None
    if in_parts:
        cuts = sorted({0, 1, chunks - 1, chunks})
        returned = []
        for start, stop in zip(cuts[:-1], cuts[1:]):
            source, coded = arrived[min(start, 1)]
            returned.append((start, stop - start, swap(*conv(start - source, stop - start, coded))))
        for start, count, coded in returned:
            out = post(start, count, out, coded)
    else:
        returned = []
        for chunk in range(chunks):
            coded, scale = pre(chunk, 1)
            coded = swap(coded.reshape(slabs, seq_count, per, B).transpose(1, 0, 2, 3))
            scale = jnp.repeat(swap(scale.reshape(seq_count, per)), slabs, axis=0)
            scale = jnp.pad(scale, ((0, 0), (0, LANES - per)))
            coded, scale = conv(0, 1, coded.reshape(A * per, B), scale)
            coded = swap(coded.reshape(seq_count, slabs, per, B))
            scale = lax.all_gather(scale[0, :per], "seq", axis=0, tiled=True)
            returned.append((coded.transpose(1, 0, 2, 3).reshape(slabs, LANES, B), scale.reshape(1, LANES)))
        for chunk, (coded, scale) in enumerate(returned):
            out = post(chunk, 1, out, coded, scale)
    return out


def solution(mesh):
    return jax.shard_map(
        per_device,
        mesh=mesh,
        in_specs=(
            P("seq", "chan"),
            P("seq", "chan"),
            P("seq", "chan"),
            P(None, None, "chan"),
            P("chan"),
            P("chan", "seq"),
        ),
        out_specs=P("seq", "chan"),
        check_vma=False,
    )
```

```python
from functools import partial

import jax
import jax.numpy as jnp
import numpy as np
from jax import lax
from jax.experimental import pallas as pl
from jax.experimental.pallas import tpu as pltpu
from jax.sharding import PartitionSpec as P

A = 256
B = 256
LANES = 128
EXTRA = 8

POWER = 15
TOP = 2.0**8.375
LEAST = 1e-34


def tables():
    index = np.arange(A)
    angle = 2.0 * np.pi / A * (np.outer(index, index) % A)
    cos, sin = np.cos(angle), -np.sin(angle)
    bf16 = jnp.bfloat16
    cos_hi, sin_hi = cos.astype(bf16), sin.astype(bf16)
    cos_lo = (cos - cos_hi.astype(np.float64)).astype(bf16)
    sin_lo = (sin - sin_hi.astype(np.float64)).astype(bf16)
    turn = 2.0 * np.pi / (A * B) * (np.outer(index, index) % (A * B))
    return cos_hi, sin_hi, cos_lo, sin_lo, np.cos(turn).astype(np.float32), np.sin(turn).astype(np.float32)


def encode(scaled):
    cube = scaled * scaled * scaled
    sixth = cube * cube
    return sixth * sixth * cube


def decode(coded):
    size = jnp.exp2(jnp.log2(jnp.abs(coded)) * (1.0 / POWER))
    return jnp.where(coded < 0, -size, size)


def split(value):
    high = value.astype(jnp.bfloat16)
    return high, (value - high.astype(jnp.float32)).astype(jnp.bfloat16)


def left_dft(left, pairs):
    high, low = split(jnp.concatenate([part for pair in pairs for part in pair], axis=1))
    out = jnp.dot(left, jnp.concatenate([high, high, low], axis=0), preferred_element_type=jnp.float32)
    result = []
    for index in range(len(pairs)):
        re, im = (out[:, (2 * index + part) * B : (2 * index + part + 1) * B] for part in range(2))
        result.append((re[:A] - im[A:], im[:A] + re[A:]))
    return result


def right_dft(right, pairs):
    pieces = []
    for re, im in pairs:
        re_hi, re_lo = split(re)
        im_hi, im_lo = split(im)
        pieces.append(jnp.concatenate([re_hi, im_hi, re_hi, im_hi, re_lo, im_lo], axis=1))
    out = jnp.dot(jnp.concatenate(pieces, axis=0), right, preferred_element_type=jnp.float32)
    return [(out[index * A : (index + 1) * A, :B], out[index * A : (index + 1) * A, B:]) for index in range(len(pairs))]


def turn(pairs, turn_re_ref, turn_im_ref):
    cos, sin = turn_re_ref[...], turn_im_ref[...]
    return [(re * cos + im * sin, im * cos - re * sin) for re, im in pairs]


def short_conv(window_ref, which, rows, taps, column):
    window_ref[which, :8, :] = window_ref[which, B:, :]
    window_ref[which, 8:, :] = rows
    return (
        taps[0, column][None, :] * rows
        + taps[1, column][None, :] * window_ref[which, 7 : 7 + B, :]
        + taps[2, column][None, :] * window_ref[which, 6 : 6 + B, :]
    )


def gate_all(key_ref, value_ref, halo_ref, taps_ref, gated_ref, window_ref):
    taps = taps_ref[...]
    for which in range(1, 3):
        before = jnp.zeros((8, LANES), jnp.float32) if halo_ref is None else halo_ref[which].astype(jnp.float32)
        window_ref[which, B:, :] = before

    def gate(slab, most):
        rows = pl.ds(pl.multiple_of(slab * B, B), B)
        key = short_conv(window_ref, 1, key_ref[rows, :].astype(jnp.float32), taps, 1)
        value = short_conv(window_ref, 2, value_ref[rows, :].astype(jnp.float32), taps, 2)
        gated = key * value
        gated_ref[rows, :] = gated
        return jnp.maximum(most, jnp.max(jnp.abs(gated).reshape(B // 8, 8, LANES), axis=0))

    most = lax.fori_loop(0, key_ref.shape[0] // B, gate, jnp.zeros((8, LANES), jnp.float32))
    return scale_of(jnp.max(most, axis=0, keepdims=True))


def scale_of(most):
    return (jnp.maximum(most, LEAST) * (1.0 / TOP)).astype(jnp.bfloat16).astype(jnp.float32)


def scale_tile(scale):
    return jnp.broadcast_to(jnp.concatenate([scale, scale], axis=1), (EXTRA, B)).astype(jnp.bfloat16)


def edges(key_ref, value_ref):
    row = lax.broadcasted_iota(jnp.int32, (8, LANES), 0)
    key_first, value_first = (ref[:8, :].astype(jnp.float32) for ref in (key_ref, value_ref))
    key_last, value_last = (ref[ref.shape[0] - 8 :, :].astype(jnp.float32) for ref in (key_ref, value_ref))
    firsts = jnp.where(row < 2, key_first, pltpu.roll(value_first, 4, axis=0))
    lasts = jnp.where(row < 6, pltpu.roll(key_last, 4, axis=0), value_last)
    return jnp.where((row < 2) | ((row >= 4) & (row < 6)), firsts, lasts)


def edge_gated(mine, before, taps):
    result = []
    for position in range(2):
        pair = []
        for which in range(2):
            base = 4 * which
            lines = [before[base + 2 : base + 3], before[base + 3 : base + 4], mine[base : base + 1], mine[base + 1 : base + 2]]
            pair.append(sum(taps[tap, 1 + which][None, :] * lines[2 + position - tap] for tap in range(3)))
        result.append(pair[0] * pair[1])
    return result


def pre_whole_kernel(key_ref, value_ref, halo_ref, taps_ref, coded_ref, scale_ref, gated_ref, window_ref):
    scale = gate_all(key_ref, value_ref, halo_ref, taps_ref, gated_ref, window_ref)
    scale_ref[...] = scale
    factor = 1.0 / scale

    def send(slab, _):
        rows = pl.ds(pl.multiple_of(slab * B, B), B)
        coded_ref[slab] = encode(gated_ref[rows, :] * factor).astype(jnp.bfloat16).T
        return 0

    lax.fori_loop(0, coded_ref.shape[0], send, 0)


def pre_parts_kernel(per, key_ref, value_ref, taps_ref, *rest):
    filter_refs, (parts_ref, gated_ref, window_ref, filter_rows_ref) = rest[:-4], rest[-4:]
    count, _, size, _ = parts_ref.shape
    slabs = key_ref.shape[0] // B
    scale = gate_all(key_ref, value_ref, None, taps_ref, gated_ref, window_ref)
    factor = 1.0 / scale

    def send(slab, _):
        rows = pl.ds(pl.multiple_of(slab * B, B), B)
        coded = encode(gated_ref[rows, :] * factor).astype(jnp.bfloat16).T
        place = pl.ds(pl.multiple_of(slab * per, per), per)
        for target in range(count):
            parts_ref[target, 0, place, :] = coded[target * per : (target + 1) * per]
        return 0

    lax.fori_loop(0, slabs, send, 0)
    tile = jnp.concatenate([jnp.broadcast_to(scale, (EXTRA, LANES)), edges(key_ref, value_ref)], axis=1).astype(jnp.bfloat16)
    for filter_ref in filter_refs:
        for slab in range(slabs):
            filter_rows_ref[slab : slab + 1, :] = filter_ref[:, slab * B : (slab + 1) * B]
        filter_rows = jnp.concatenate(split(filter_rows_ref[...]), axis=0)
        for target in range(count):
            parts_ref[target, 0, slabs * per : size - EXTRA, :] = filter_rows
    for target in range(count):
        parts_ref[target, 0, size - EXTRA :, :] = tile


def parts_spectrum_kernel(parts_ref, *refs):
    *refs, filter_ref = refs
    slabs = parts_ref.shape[2] // 2
    for source in range(parts_ref.shape[0]):
        both = parts_ref[source, 0].astype(jnp.float32)
        filter_ref[source * slabs : (source + 1) * slabs, :] = both[:slabs] + both[slabs:]
    spectrum_kernel(filter_ref, *refs)


def spectrum_kernel(filter_ref, *refs):
    cos_hi, sin_hi, cos_lo, sin_lo = (ref[...] for ref in refs[:4])
    turn_re_ref, turn_im_ref, re_ref, im_ref, left_ref, right_ref = refs[4:]
    for piece, (cos, sin) in enumerate(((cos_hi, sin_hi), (cos_lo, sin_lo), (cos_hi, sin_hi))):
        left_ref[:A, piece * A : (piece + 1) * A] = cos
        left_ref[A:, piece * A : (piece + 1) * A] = sin
        right_ref[2 * piece * B : (2 * piece + 1) * B, :B] = cos
        right_ref[2 * piece * B : (2 * piece + 1) * B, B:] = sin
        right_ref[(2 * piece + 1) * B : (2 * piece + 2) * B, :B] = -sin
        right_ref[(2 * piece + 1) * B : (2 * piece + 2) * B, B:] = cos
    taps = filter_ref[...]
    pairs = left_dft(left_ref[...], [(taps, jnp.zeros_like(taps))])
    ((re, im),) = right_dft(right_ref[...], turn(pairs, turn_re_ref, turn_im_ref))
    re_ref[...] = re * (1.0 / (A * B))
    im_ref[...] = im * (1.0 / (A * B))


def put(work_ref, rows, value):
    for part in range(2):
        work_ref[part, rows, :] = value[:, part * LANES : (part + 1) * LANES]


def take(work_ref, rows):
    return jnp.concatenate([work_ref[part, rows, :] for part in range(2)], axis=1)


def convolve_all(per, base, scale_ref, left_ref, right_ref, turn_re_ref, turn_im_ref, spec_re_ref, spec_im_ref, work_ref):
    lane = lax.broadcasted_iota(jnp.int32, (A, LANES), 1)
    row_lane = lax.broadcasted_iota(jnp.int32, (1, LANES), 1)

    def signal(channel):
        scale = jnp.sum(jnp.where(lane == base + channel, scale_ref[...], 0.0), axis=1, keepdims=True)
        return take(work_ref, pl.ds(channel, A, stride=per)) * scale

    def emit(channel, value, scales):
        scale = scale_of(jnp.max(jnp.abs(value), keepdims=True))
        put(work_ref, pl.ds(channel, A, stride=per), encode(value * (1.0 / scale)))
        return jnp.where(row_lane == base + channel, scale, scales)

    together = 2 if per % 4 == 0 else 1

    def convolve(index, scales):
        first = 2 * together * index
        pairs = [(signal(first + 2 * which), signal(first + 2 * which + 1)) for which in range(together)]
        pairs = turn(left_dft(left_ref[...], pairs), turn_re_ref, turn_im_ref)
        pairs = right_dft(right_ref[...], pairs)
        spec_re, spec_im = spec_re_ref[...], spec_im_ref[...]
        pairs = [(re * spec_re - im * spec_im, -(re * spec_im + im * spec_re)) for re, im in pairs]
        pairs = turn(right_dft(right_ref[...], pairs), turn_re_ref, turn_im_ref)
        pairs = left_dft(left_ref[...], pairs)
        for which, (re, im) in enumerate(pairs):
            scales = emit(first + 2 * which, re, scales)
            scales = emit(first + 2 * which + 1, -im, scales)
        return scales

    return lax.fori_loop(0, per // (2 * together), convolve, jnp.zeros((1, LANES), jnp.float32))


def conv_whole_kernel(coded_ref, scale_ref, *rest):
    constants, (out_ref, out_scale_ref, work_ref) = rest[:6], rest[6:]
    per = coded_ref.shape[0] // A

    def receive(slab, _):
        rows = pl.ds(pl.multiple_of(slab * A, A), A)
        put(work_ref, rows, decode(coded_ref[rows, :].astype(jnp.float32)))
        return 0

    lax.fori_loop(0, per, receive, 0)
    scales = convolve_all(per, 0, scale_ref, *constants, work_ref)
    out_scale_ref[...] = jnp.broadcast_to(scales, out_scale_ref.shape)

    def send(slab, _):
        rows = pl.ds(pl.multiple_of(slab * A, A), A)
        out_ref[rows, :] = take(work_ref, rows).astype(jnp.bfloat16)
        return 0

    lax.fori_loop(0, per, send, 0)


def conv_parts_kernel(per, place_ref, parts_ref, taps_ref, *rest):
    sources, (out_ref, work_ref, scale_ref, edge_ref), constants, sems = rest[:6], rest[6:10], rest[10:16], rest[16]
    copies = [pltpu.make_async_copy(*pair, sems.at[index]) for index, pair in enumerate(zip(sources, constants))]

    @pl.when(pl.program_id(0) == 0)
    def _():
        for copy in copies:
            copy.start()

    count, _, size, _ = parts_ref.shape
    out_size = out_ref.shape[2]
    slabs = A // count
    block = slabs * per
    steps = block // A

    def receive(index, _):
        for step in range(steps):
            value = parts_ref[index, 0, step * A : (step + 1) * A, :].astype(jnp.float32)
            put(work_ref, pl.ds(pl.multiple_of(index * block + step * A, A), A), decode(value))
        row = parts_ref[index, 0, size - EXTRA :, :LANES].astype(jnp.float32)[:1]
        scale_ref[pl.ds(pl.multiple_of(index * slabs, slabs), slabs), :] = jnp.broadcast_to(row, (slabs, LANES))
        return 0

    lax.fori_loop(0, count, receive, 0)

    taps = taps_ref[...]
    edge_ref[...] = jnp.zeros_like(edge_ref)
    before = jnp.zeros((EXTRA, LANES), jnp.float32)
    for index in range(count):
        end = parts_ref[index, 0, size - EXTRA :, :].astype(jnp.float32)
        mine = end[:, LANES:]
        for position, gated in enumerate(edge_gated(mine, before, taps)):
            edge_ref[2 * index + position : 2 * index + position + 1, :] = gated / end[:1, :LANES]
        before = mine
    edge_ref[...] = edge_ref[...].T
    fixed = edge_ref[pl.ds(pl.multiple_of(place_ref[0] * per, per), per), :]
    lane = lax.broadcasted_iota(jnp.int32, (per, LANES), 1)
    for index in range(count):
        rows = slice(index * block, index * block + per)
        moved = pltpu.roll(fixed, (LANES - 2 * index) % LANES, axis=1)
        work_ref[0, rows, :] = jnp.where(lane < 2, moved, work_ref[0, rows, :])

    @pl.when(pl.program_id(0) == 0)
    def _():
        for copy in copies:
            copy.wait()

    tile = scale_tile(convolve_all(per, place_ref[0] * per, scale_ref, *constants, work_ref))

    def send(index, _):
        for step in range(steps):
            value = take(work_ref, pl.ds(pl.multiple_of(index * block + step * A, A), A))
            out_ref[index, 0, step * A : (step + 1) * A, :] = value.astype(jnp.bfloat16)
        out_ref[index, 0, out_size - EXTRA :, :] = tile
        return 0

    lax.fori_loop(0, count, send, 0)


def mix_all(step, query_ref, key_ref, value_ref, halo_ref, taps_ref, skip_ref, convolved_of, out_ref, window_ref):
    taps = taps_ref[...]

    @pl.when(step == 0)
    def _():
        for which in range(3):
            window_ref[which, B:, :] = halo_ref[which].astype(jnp.float32)

    def mix(slab, _):
        rows = pl.ds(pl.multiple_of(slab * B, B), B)
        query, key, value = (
            short_conv(window_ref, which, ref[rows, :].astype(jnp.float32), taps, which)
            for which, ref in enumerate((query_ref, key_ref, value_ref))
        )
        out_ref[rows, :] = query * (convolved_of(slab) + skip_ref[...] * (key * value))
        return 0

    lax.fori_loop(0, query_ref.shape[0] // B, mix, 0)


def post_whole_kernel(*refs):
    inputs, (coded_ref, scale_ref), (out_ref, window_ref) = refs[:6], refs[6:8], refs[-2:]

    def convolved_of(slab):
        return decode(coded_ref[slab].T.astype(jnp.float32)) * scale_ref[...]

    mix_all(pl.program_id(0), *inputs, convolved_of, out_ref, window_ref)


def post_parts_kernel(*refs):
    inputs, (parts_ref, ends_ref), (out_ref, window_ref) = refs[:6], refs[6:8], refs[-2:]
    count = parts_ref.shape[0]
    per = LANES // count
    scale = jnp.zeros((EXTRA, LANES), jnp.float32)
    for source in range(count):
        scale = scale + ends_ref[source, 0].astype(jnp.float32)[:, :LANES]
    scale = scale[:1]

    def convolved_of(slab):
        place = pl.ds(pl.multiple_of(slab * per, per), per)
        coded = jnp.concatenate([parts_ref[source, 0, place, :] for source in range(count)], axis=0)
        return decode(coded.T.astype(jnp.float32)) * scale

    mix_all(pl.program_id(1), *inputs, convolved_of, out_ref, window_ref)


def params():
    return pltpu.CompilerParams(vmem_limit_bytes=48 * 1024 * 1024)


def cost(flops, size):
    return pl.CostEstimate(flops=flops // 1000, bytes_accessed=size // 1000, transcendentals=0)


SCALAR = pl.BlockSpec(memory_space=pltpu.SMEM)


def per_device(query_proj, key_proj, value_proj, short_taps, skip_gain, long_filter):
    tok_count, chan_width = query_proj.shape
    seq_count = lax.axis_size("seq")
    slabs = tok_count // B
    chunks = chan_width // LANES
    per = LANES // seq_count
    in_parts = per % 16 == 0 and (slabs * per) % A == 0 and slabs % 8 == 0 and seq_count & (seq_count - 1) == 0
    size = slabs * per + EXTRA
    place = lax.axis_index("seq").astype(jnp.int32).reshape(1)

    ends = jnp.stack([query_proj[-8:], key_proj[-8:], value_proj[-8:]])
    halo = lax.ppermute(ends, "seq", [(source, source + 1) for source in range(seq_count - 1)])
    skip_row = skip_gain[None, :]

    swap = partial(lax.all_to_all, axis_name="seq", split_axis=0, concat_axis=0, tiled=True)

    def whole_block(shape):
        return pl.BlockSpec(shape, lambda i: (0,) * len(shape))

    def pre(chunk, count, *filters):
        rows = pl.BlockSpec((tok_count, LANES), lambda i: (0, chunk + i))
        if in_parts:
            rows_out = size + 2 * slabs * len(filters)
            out_shape = [jax.ShapeDtypeStruct((seq_count, count, rows_out, B), jnp.bfloat16)]
            out_specs = [pl.BlockSpec((seq_count, 1, rows_out, B), lambda i: (0, i, 0, 0))]
        else:
            out_shape = [
                jax.ShapeDtypeStruct((slabs, LANES, B), jnp.bfloat16),
                jax.ShapeDtypeStruct((1, LANES), jnp.float32),
            ]
            out_specs = [whole_block(out.shape) for out in out_shape]
        return pl.pallas_call(
            partial(pre_parts_kernel, per) if in_parts else pre_whole_kernel,
            grid=(count,),
            in_specs=[rows, rows]
            + [pl.BlockSpec((3, 8, LANES), lambda i: (0, 0, chunk + i))] * (not in_parts)
            + [pl.BlockSpec((3, 3, LANES), lambda i: (0, 0, chunk + i))]
            + [whole_block((1, tok_count))] * len(filters),
            out_specs=out_specs,
            out_shape=out_shape,
            scratch_shapes=[pltpu.VMEM((tok_count, LANES), jnp.float32), pltpu.VMEM((3, 8 + B, LANES), jnp.float32)]
            + [pltpu.VMEM((slabs, B), jnp.float32)] * in_parts,
            compiler_params=params(),
            cost_estimate=cost(count * 40 * tok_count * LANES, count * 6 * tok_count * LANES),
            name="pre",
        )(key_proj, value_proj, *[halo] * (not in_parts), short_taps, *filters)

    def conv(start, first, count, coded, *scale):
        rows = A * per
        args = (coded, *scale, left, right, turn_re, turn_im, spec_re, spec_im)
        in_specs = [whole_block(arg.shape) for arg in args]
        scratch = [pltpu.VMEM((2, rows, LANES), jnp.float32)]
        if in_parts:
            args = (place, coded, short_taps) + args[1:]
            block = (seq_count, 1, coded.shape[2], B)
            in_specs = [SCALAR, pl.BlockSpec(block, lambda i: (0, first + i, 0, 0))]
            in_specs.append(pl.BlockSpec((3, 3, LANES), lambda i: (0, 0, start + i)))
            in_specs += [pl.BlockSpec(memory_space=pltpu.HBM)] * 6
            out_shape = [jax.ShapeDtypeStruct((seq_count, count, size, B), jnp.bfloat16)]
            out_specs = [pl.BlockSpec((seq_count, 1, size, B), lambda i: (0, i, 0, 0))]
            scratch += [pltpu.VMEM((A, LANES), jnp.float32), pltpu.VMEM((LANES, LANES), jnp.float32)]
            scratch += [pltpu.VMEM(arg.shape, arg.dtype) for arg in args[3:]] + [pltpu.SemaphoreType.DMA((6,))]
        else:
            out_shape = [
                jax.ShapeDtypeStruct((rows, B), jnp.bfloat16),
                jax.ShapeDtypeStruct((8, LANES), jnp.float32),
            ]
            out_specs = [whole_block(out.shape) for out in out_shape]
        return pl.pallas_call(
            partial(conv_parts_kernel, per) if in_parts else conv_whole_kernel,
            grid=(count,),
            in_specs=in_specs,
            out_specs=out_specs,
            out_shape=out_shape,
            scratch_shapes=scratch,
            compiler_params=params(),
            cost_estimate=cost(count * per // 2 * 4 * 2 * 512 * 1536 * 256, count * 4 * rows * B),
            name="conv",
        )(*args)

    def post(chunk, count, out, coded, *scale):
        step = min(2048, tok_count)
        block = step // B
        rows = pl.BlockSpec((step, LANES), lambda u, i: (i, chunk + u))
        in_specs = [
            rows,
            rows,
            rows,
            pl.BlockSpec((3, 8, LANES), lambda u, i: (0, 0, chunk + u)),
            pl.BlockSpec((3, 3, LANES), lambda u, i: (0, 0, chunk + u)),
            pl.BlockSpec((1, LANES), lambda u, i: (0, chunk + u)),
        ]
        args = [query_proj, key_proj, value_proj, halo, short_taps, skip_row]
        if in_parts:
            last = slabs * per // EXTRA
            in_specs += [
                pl.BlockSpec((seq_count, 1, block * per, B), lambda u, i: (0, u, i, 0)),
                pl.BlockSpec((seq_count, 1, EXTRA, B), lambda u, i: (0, u, last, 0)),
            ]
            args += [coded, coded]
        else:
            in_specs += [
                pl.BlockSpec((block, LANES, B), lambda u, i: (i, 0, 0)),
                pl.BlockSpec((1, LANES), lambda u, i: (0, 0)),
            ]
            args += [coded, *scale]
        if out is not None:
            in_specs.append(pl.BlockSpec(memory_space=pl.ANY))
            args.append(out)
        return pl.pallas_call(
            post_parts_kernel if in_parts else post_whole_kernel,
            grid=(count, tok_count // step),
            in_specs=in_specs,
            out_specs=rows,
            out_shape=jax.ShapeDtypeStruct((tok_count, chan_width), jnp.float32),
            scratch_shapes=[pltpu.VMEM((3, 8 + B, LANES), jnp.float32)],
            input_output_aliases={} if out is None else {len(args) - 1: 0},
            compiler_params=params(),
            cost_estimate=cost(count * 60 * tok_count * LANES, count * 12 * tok_count * LANES),
            name="post",
        )(*args)

    if in_parts:
        arrived = [(0, swap(*pre(0, 1, long_filter)))]
        if chunks > 1:
            arrived.append((1, swap(*pre(1, chunks - 1))))
        whole_filter = arrived[0][1]
        filter_spec = pl.BlockSpec((seq_count, 1, 2 * slabs, B), lambda i: (0, 0, per // 2, 0))
    else:
        whole_filter = swap(jnp.broadcast_to(long_filter.reshape(slabs, B), (seq_count, slabs, B))).reshape(A, B)
        filter_spec = whole_block((A, B))
    cos_hi, sin_hi, cos_lo, sin_lo, turn_re, turn_im = (jnp.asarray(table) for table in tables())
    filter_args = (whole_filter, cos_hi, sin_hi, cos_lo, sin_lo, turn_re, turn_im)
    spec_shape = [jax.ShapeDtypeStruct((A, B), jnp.float32)] * 2
    spec_shape += [jax.ShapeDtypeStruct((2 * A, 3 * A), jnp.bfloat16), jax.ShapeDtypeStruct((6 * B, 2 * B), jnp.bfloat16)]
    spec_re, spec_im, left, right = pl.pallas_call(
        parts_spectrum_kernel if in_parts else spectrum_kernel,
        grid=(1,),
        in_specs=[filter_spec] + [whole_block((A, B))] * 6,
        out_specs=[whole_block(out.shape) for out in spec_shape],
        out_shape=spec_shape,
        scratch_shapes=[pltpu.VMEM((A, B), jnp.float32)] * in_parts,
        compiler_params=params(),
        cost_estimate=cost(2 * 2 * 512 * 1536 * 256, 16 * A * B),
        name="spectrum",
    )(*filter_args)

    out = None
    if in_parts:
        cuts = sorted({0, 1, chunks - 1, chunks})
        returned = []
        for start, stop in zip(cuts[:-1], cuts[1:]):
            source, coded = arrived[min(start, 1)]
            (coded,) = conv(start, start - source, stop - start, coded)
            if start == 0:
                coded, halo = lax.optimization_barrier((coded, halo))
            returned.append((start, stop - start, swap(coded)))
        for start, count, coded in returned:
            out = post(start, count, out, coded)
    else:
        returned = []
        for chunk in range(chunks):
            coded, scale = pre(chunk, 1)
            coded = swap(coded.reshape(slabs, seq_count, per, B).transpose(1, 0, 2, 3))
            scale = jnp.repeat(swap(scale.reshape(seq_count, per)), slabs, axis=0)
            scale = jnp.pad(scale, ((0, 0), (0, LANES - per)))
            coded, scale = conv(chunk, 0, 1, coded.reshape(A * per, B), scale)
            coded = swap(coded.reshape(seq_count, slabs, per, B))
            scale = lax.all_gather(scale[0, :per], "seq", axis=0, tiled=True)
            returned.append((coded.transpose(1, 0, 2, 3).reshape(slabs, LANES, B), scale.reshape(1, LANES)))
        for chunk, (coded, scale) in enumerate(returned):
            out = post(chunk, 1, out, coded, scale)
    return out


def solution(mesh):
    return jax.shard_map(
        per_device,
        mesh=mesh,
        in_specs=(
            P("seq", "chan"),
            P("seq", "chan"),
            P("seq", "chan"),
            P(None, None, "chan"),
            P("chan"),
            P("chan", "seq"),
        ),
        out_specs=P("seq", "chan"),
        check_vma=False,
    )
```

```python
from functools import partial

import jax
import jax.numpy as jnp
import numpy as np
from jax import lax
from jax.experimental import pallas as pl
from jax.experimental.pallas import tpu as pltpu
from jax.sharding import PartitionSpec as P

A = 256
B = 256
LANES = 128
EXTRA = 8

POWER = 15
TOP = 2.0**8.375
LEAST = 1e-34


def tables():
    index = np.arange(A)
    angle = 2.0 * np.pi / A * (np.outer(index, index) % A)
    cos, sin = np.cos(angle), -np.sin(angle)
    bf16 = jnp.bfloat16
    cos_hi, sin_hi = cos.astype(bf16), sin.astype(bf16)
    cos_lo = (cos - cos_hi.astype(np.float64)).astype(bf16)
    sin_lo = (sin - sin_hi.astype(np.float64)).astype(bf16)
    turn = 2.0 * np.pi / (A * B) * (np.outer(index, index) % (A * B))
    return cos_hi, sin_hi, cos_lo, sin_lo, np.cos(turn).astype(np.float32), np.sin(turn).astype(np.float32)


def encode(scaled):
    cube = scaled * scaled * scaled
    sixth = cube * cube
    return sixth * sixth * cube


def decode(coded):
    size = jnp.exp2(jnp.log2(jnp.abs(coded)) * (1.0 / POWER))
    return jnp.where(coded < 0, -size, size)


def split(value):
    high = value.astype(jnp.bfloat16)
    return high, (value - high.astype(jnp.float32)).astype(jnp.bfloat16)


def left_dft(left, pairs):
    high, low = split(jnp.concatenate([part for pair in pairs for part in pair], axis=1))
    out = jnp.dot(left, jnp.concatenate([high, high, low], axis=0), preferred_element_type=jnp.float32)
    result = []
    for index in range(len(pairs)):
        re, im = (out[:, (2 * index + part) * B : (2 * index + part + 1) * B] for part in range(2))
        result.append((re[:A] - im[A:], im[:A] + re[A:]))
    return result


def right_dft(right, pairs):
    pieces = []
    for re, im in pairs:
        re_hi, re_lo = split(re)
        im_hi, im_lo = split(im)
        pieces.append(jnp.concatenate([re_hi, im_hi, re_hi, im_hi, re_lo, im_lo], axis=1))
    out = jnp.dot(jnp.concatenate(pieces, axis=0), right, preferred_element_type=jnp.float32)
    return [(out[index * A : (index + 1) * A, :B], out[index * A : (index + 1) * A, B:]) for index in range(len(pairs))]


def turn(pairs, turn_re_ref, turn_im_ref):
    cos, sin = turn_re_ref[...], turn_im_ref[...]
    return [(re * cos + im * sin, im * cos - re * sin) for re, im in pairs]


def short_conv(window_ref, which, rows, taps, column):
    window_ref[which, :8, :] = window_ref[which, B:, :]
    window_ref[which, 8:, :] = rows
    return (
        taps[0, column][None, :] * rows
        + taps[1, column][None, :] * window_ref[which, 7 : 7 + B, :]
        + taps[2, column][None, :] * window_ref[which, 6 : 6 + B, :]
    )


def gate_all(key_ref, value_ref, halo_ref, taps_ref, gated_ref, window_ref):
    taps = taps_ref[...]
    for which in range(1, 3):
        before = jnp.zeros((8, LANES), jnp.float32) if halo_ref is None else halo_ref[which].astype(jnp.float32)
        window_ref[which, B:, :] = before

    def gate(slab, most):
        rows = pl.ds(pl.multiple_of(slab * B, B), B)
        key = short_conv(window_ref, 1, key_ref[rows, :].astype(jnp.float32), taps, 1)
        value = short_conv(window_ref, 2, value_ref[rows, :].astype(jnp.float32), taps, 2)
        gated = key * value
        gated_ref[rows, :] = gated
        return jnp.maximum(most, jnp.max(jnp.abs(gated).reshape(B // 8, 8, LANES), axis=0))

    most = lax.fori_loop(0, key_ref.shape[0] // B, gate, jnp.zeros((8, LANES), jnp.float32))
    return scale_of(jnp.max(most, axis=0, keepdims=True))


def scale_of(most):
    return (jnp.maximum(most, LEAST) * (1.0 / TOP)).astype(jnp.bfloat16).astype(jnp.float32)


def scale_tile(scale):
    return jnp.broadcast_to(jnp.concatenate([scale, scale], axis=1), (EXTRA, B)).astype(jnp.bfloat16)


def edges(key_ref, value_ref):
    row = lax.broadcasted_iota(jnp.int32, (8, LANES), 0)
    key_first, value_first = (ref[:8, :].astype(jnp.float32) for ref in (key_ref, value_ref))
    key_last, value_last = (ref[ref.shape[0] - 8 :, :].astype(jnp.float32) for ref in (key_ref, value_ref))
    firsts = jnp.where(row < 2, key_first, pltpu.roll(value_first, 4, axis=0))
    lasts = jnp.where(row < 6, pltpu.roll(key_last, 4, axis=0), value_last)
    return jnp.where((row < 2) | ((row >= 4) & (row < 6)), firsts, lasts)


def edge_gated(mine, before, taps):
    result = []
    for position in range(2):
        pair = []
        for which in range(2):
            base = 4 * which
            lines = [before[base + 2 : base + 3], before[base + 3 : base + 4], mine[base : base + 1], mine[base + 1 : base + 2]]
            pair.append(sum(taps[tap, 1 + which][None, :] * lines[2 + position - tap] for tap in range(3)))
        result.append(pair[0] * pair[1])
    return result


def pre_whole_kernel(key_ref, value_ref, halo_ref, taps_ref, coded_ref, scale_ref, gated_ref, window_ref):
    scale = gate_all(key_ref, value_ref, halo_ref, taps_ref, gated_ref, window_ref)
    scale_ref[...] = scale
    factor = 1.0 / scale

    def send(slab, _):
        rows = pl.ds(pl.multiple_of(slab * B, B), B)
        coded_ref[slab] = encode(gated_ref[rows, :] * factor).astype(jnp.bfloat16).T
        return 0

    lax.fori_loop(0, coded_ref.shape[0], send, 0)


def pre_parts_kernel(per, key_ref, value_ref, taps_ref, *rest):
    filter_refs, (parts_ref, gated_ref, window_ref, filter_rows_ref) = rest[:-4], rest[-4:]
    count, _, size, _ = parts_ref.shape
    slabs = key_ref.shape[0] // B
    scale = gate_all(key_ref, value_ref, None, taps_ref, gated_ref, window_ref)
    factor = 1.0 / scale

    def send(slab, _):
        rows = pl.ds(pl.multiple_of(slab * B, B), B)
        coded = encode(gated_ref[rows, :] * factor).astype(jnp.bfloat16).T
        place = pl.ds(pl.multiple_of(slab * per, per), per)
        for target in range(count):
            parts_ref[target, 0, place, :] = coded[target * per : (target + 1) * per]
        return 0

    lax.fori_loop(0, slabs, send, 0)
    tile = jnp.concatenate([jnp.broadcast_to(scale, (EXTRA, LANES)), edges(key_ref, value_ref)], axis=1).astype(jnp.bfloat16)
    for filter_ref in filter_refs:
        for slab in range(slabs):
            filter_rows_ref[slab : slab + 1, :] = filter_ref[:, slab * B : (slab + 1) * B]
        filter_rows = jnp.concatenate(split(filter_rows_ref[...]), axis=0)
        for target in range(count):
            parts_ref[target, 0, slabs * per : size - EXTRA, :] = filter_rows
    for target in range(count):
        parts_ref[target, 0, size - EXTRA :, :] = tile


def parts_spectrum_kernel(parts_ref, *refs):
    *refs, filter_ref = refs
    slabs = parts_ref.shape[2] // 2
    for source in range(parts_ref.shape[0]):
        both = parts_ref[source, 0].astype(jnp.float32)
        filter_ref[source * slabs : (source + 1) * slabs, :] = both[:slabs] + both[slabs:]
    spectrum_kernel(filter_ref, *refs)


def spectrum_kernel(filter_ref, *refs):
    cos_hi, sin_hi, cos_lo, sin_lo = (ref[...] for ref in refs[:4])
    turn_re_ref, turn_im_ref, re_ref, im_ref, left_ref, right_ref = refs[4:]
    for piece, (cos, sin) in enumerate(((cos_hi, sin_hi), (cos_lo, sin_lo), (cos_hi, sin_hi))):
        left_ref[:A, piece * A : (piece + 1) * A] = cos
        left_ref[A:, piece * A : (piece + 1) * A] = sin
        right_ref[2 * piece * B : (2 * piece + 1) * B, :B] = cos
        right_ref[2 * piece * B : (2 * piece + 1) * B, B:] = sin
        right_ref[(2 * piece + 1) * B : (2 * piece + 2) * B, :B] = -sin
        right_ref[(2 * piece + 1) * B : (2 * piece + 2) * B, B:] = cos
    taps = filter_ref[...]
    pairs = left_dft(left_ref[...], [(taps, jnp.zeros_like(taps))])
    ((re, im),) = right_dft(right_ref[...], turn(pairs, turn_re_ref, turn_im_ref))
    re_ref[...] = re * (1.0 / (A * B))
    im_ref[...] = im * (1.0 / (A * B))


def put(work_ref, rows, value):
    for part in range(2):
        work_ref[part, rows, :] = value[:, part * LANES : (part + 1) * LANES]


def take(work_ref, rows):
    return jnp.concatenate([work_ref[part, rows, :] for part in range(2)], axis=1)


def convolve_all(per, base, scale_ref, left_ref, right_ref, turn_re_ref, turn_im_ref, spec_re_ref, spec_im_ref, work_ref):
    lane = lax.broadcasted_iota(jnp.int32, (A, LANES), 1)
    row_lane = lax.broadcasted_iota(jnp.int32, (1, LANES), 1)

    def signal(channel):
        scale = jnp.sum(jnp.where(lane == base + channel, scale_ref[...], 0.0), axis=1, keepdims=True)
        return take(work_ref, pl.ds(channel, A, stride=per)) * scale

    def emit(channel, value, scales):
        scale = scale_of(jnp.max(jnp.abs(value), keepdims=True))
        put(work_ref, pl.ds(channel, A, stride=per), encode(value * (1.0 / scale)))
        return jnp.where(row_lane == base + channel, scale, scales)

    together = 4 if per % 8 == 0 else 2 if per % 4 == 0 else 1

    def convolve(index, scales):
        first = 2 * together * index
        pairs = [(signal(first + 2 * which), signal(first + 2 * which + 1)) for which in range(together)]
        pairs = turn(left_dft(left_ref[...], pairs), turn_re_ref, turn_im_ref)
        pairs = right_dft(right_ref[...], pairs)
        spec_re, spec_im = spec_re_ref[...], spec_im_ref[...]
        pairs = [(re * spec_re - im * spec_im, -(re * spec_im + im * spec_re)) for re, im in pairs]
        pairs = turn(right_dft(right_ref[...], pairs), turn_re_ref, turn_im_ref)
        pairs = left_dft(left_ref[...], pairs)
        for which, (re, im) in enumerate(pairs):
            scales = emit(first + 2 * which, re, scales)
            scales = emit(first + 2 * which + 1, -im, scales)
        return scales

    return lax.fori_loop(0, per // (2 * together), convolve, jnp.zeros((1, LANES), jnp.float32))


def conv_whole_kernel(coded_ref, scale_ref, *rest):
    constants, (out_ref, out_scale_ref, work_ref) = rest[:6], rest[6:]
    per = coded_ref.shape[0] // A

    def receive(slab, _):
        rows = pl.ds(pl.multiple_of(slab * A, A), A)
        put(work_ref, rows, decode(coded_ref[rows, :].astype(jnp.float32)))
        return 0

    lax.fori_loop(0, per, receive, 0)
    scales = convolve_all(per, 0, scale_ref, *constants, work_ref)
    out_scale_ref[...] = jnp.broadcast_to(scales, out_scale_ref.shape)

    def send(slab, _):
        rows = pl.ds(pl.multiple_of(slab * A, A), A)
        out_ref[rows, :] = take(work_ref, rows).astype(jnp.bfloat16)
        return 0

    lax.fori_loop(0, per, send, 0)


def conv_parts_kernel(per, place_ref, parts_ref, taps_ref, *rest):
    sources, (out_ref, work_ref, scale_ref, edge_ref), constants, sems = rest[:6], rest[6:10], rest[10:16], rest[16]
    copies = [pltpu.make_async_copy(*pair, sems.at[index]) for index, pair in enumerate(zip(sources, constants))]

    @pl.when(pl.program_id(0) == 0)
    def _():
        for copy in copies:
            copy.start()

    count, _, size, _ = parts_ref.shape
    out_size = out_ref.shape[2]
    slabs = A // count
    block = slabs * per
    steps = block // A

    def receive(index, _):
        for step in range(steps):
            value = parts_ref[index, 0, step * A : (step + 1) * A, :].astype(jnp.float32)
            put(work_ref, pl.ds(pl.multiple_of(index * block + step * A, A), A), decode(value))
        row = parts_ref[index, 0, size - EXTRA :, :LANES].astype(jnp.float32)[:1]
        scale_ref[pl.ds(pl.multiple_of(index * slabs, slabs), slabs), :] = jnp.broadcast_to(row, (slabs, LANES))
        return 0

    lax.fori_loop(0, count, receive, 0)

    taps = taps_ref[...]
    edge_ref[...] = jnp.zeros_like(edge_ref)
    before = jnp.zeros((EXTRA, LANES), jnp.float32)
    for index in range(count):
        end = parts_ref[index, 0, size - EXTRA :, :].astype(jnp.float32)
        mine = end[:, LANES:]
        for position, gated in enumerate(edge_gated(mine, before, taps)):
            edge_ref[2 * index + position : 2 * index + position + 1, :] = gated / end[:1, :LANES]
        before = mine
    edge_ref[...] = edge_ref[...].T
    fixed = edge_ref[pl.ds(pl.multiple_of(place_ref[0] * per, per), per), :]
    lane = lax.broadcasted_iota(jnp.int32, (per, LANES), 1)
    for index in range(count):
        rows = slice(index * block, index * block + per)
        moved = pltpu.roll(fixed, (LANES - 2 * index) % LANES, axis=1)
        work_ref[0, rows, :] = jnp.where(lane < 2, moved, work_ref[0, rows, :])

    @pl.when(pl.program_id(0) == 0)
    def _():
        for copy in copies:
            copy.wait()

    tile = scale_tile(convolve_all(per, place_ref[0] * per, scale_ref, *constants, work_ref))

    def send(index, _):
        for step in range(steps):
            value = take(work_ref, pl.ds(pl.multiple_of(index * block + step * A, A), A))
            out_ref[index, 0, step * A : (step + 1) * A, :] = value.astype(jnp.bfloat16)
        out_ref[index, 0, out_size - EXTRA :, :] = tile
        return 0

    lax.fori_loop(0, count, send, 0)


def mix_all(step, query_ref, key_ref, value_ref, halo_ref, taps_ref, skip_ref, convolved_of, out_ref, window_ref):
    taps = taps_ref[...]

    @pl.when(step == 0)
    def _():
        for which in range(3):
            window_ref[which, B:, :] = halo_ref[which].astype(jnp.float32)

    def mix(slab, _):
        rows = pl.ds(pl.multiple_of(slab * B, B), B)
        query, key, value = (
            short_conv(window_ref, which, ref[rows, :].astype(jnp.float32), taps, which)
            for which, ref in enumerate((query_ref, key_ref, value_ref))
        )
        out_ref[rows, :] = query * (convolved_of(slab) + skip_ref[...] * (key * value))
        return 0

    lax.fori_loop(0, query_ref.shape[0] // B, mix, 0)


def post_whole_kernel(*refs):
    inputs, (coded_ref, scale_ref), (out_ref, window_ref) = refs[:6], refs[6:8], refs[-2:]

    def convolved_of(slab):
        return decode(coded_ref[slab].T.astype(jnp.float32)) * scale_ref[...]

    mix_all(pl.program_id(0), *inputs, convolved_of, out_ref, window_ref)


def post_parts_kernel(*refs):
    inputs, (parts_ref, ends_ref), (out_ref, window_ref) = refs[:6], refs[6:8], refs[-2:]
    count = parts_ref.shape[0]
    per = LANES // count
    scale = jnp.zeros((EXTRA, LANES), jnp.float32)
    for source in range(count):
        scale = scale + ends_ref[source, 0].astype(jnp.float32)[:, :LANES]
    scale = scale[:1]

    def convolved_of(slab):
        place = pl.ds(pl.multiple_of(slab * per, per), per)
        coded = jnp.concatenate([parts_ref[source, 0, place, :] for source in range(count)], axis=0)
        return decode(coded.T.astype(jnp.float32)) * scale

    mix_all(pl.program_id(1), *inputs, convolved_of, out_ref, window_ref)


def params():
    return pltpu.CompilerParams(vmem_limit_bytes=48 * 1024 * 1024)


def cost(flops, size):
    return pl.CostEstimate(flops=flops // 1000, bytes_accessed=size // 1000, transcendentals=0)


SCALAR = pl.BlockSpec(memory_space=pltpu.SMEM)


def per_device(query_proj, key_proj, value_proj, short_taps, skip_gain, long_filter):
    tok_count, chan_width = query_proj.shape
    seq_count = lax.axis_size("seq")
    slabs = tok_count // B
    chunks = chan_width // LANES
    per = LANES // seq_count
    in_parts = per % 16 == 0 and (slabs * per) % A == 0 and slabs % 8 == 0 and seq_count & (seq_count - 1) == 0
    size = slabs * per + EXTRA
    place = lax.axis_index("seq").astype(jnp.int32).reshape(1)

    ends = jnp.stack([query_proj[-8:], key_proj[-8:], value_proj[-8:]])
    halo = lax.ppermute(ends, "seq", [(source, source + 1) for source in range(seq_count - 1)])
    skip_row = skip_gain[None, :]

    swap = partial(lax.all_to_all, axis_name="seq", split_axis=0, concat_axis=0, tiled=True)

    def whole_block(shape):
        return pl.BlockSpec(shape, lambda i: (0,) * len(shape))

    def pre(chunk, count, *filters):
        rows = pl.BlockSpec((tok_count, LANES), lambda i: (0, chunk + i))
        if in_parts:
            rows_out = size + 2 * slabs * len(filters)
            out_shape = [jax.ShapeDtypeStruct((seq_count, count, rows_out, B), jnp.bfloat16)]
            out_specs = [pl.BlockSpec((seq_count, 1, rows_out, B), lambda i: (0, i, 0, 0))]
        else:
            out_shape = [
                jax.ShapeDtypeStruct((slabs, LANES, B), jnp.bfloat16),
                jax.ShapeDtypeStruct((1, LANES), jnp.float32),
            ]
            out_specs = [whole_block(out.shape) for out in out_shape]
        return pl.pallas_call(
            partial(pre_parts_kernel, per) if in_parts else pre_whole_kernel,
            grid=(count,),
            in_specs=[rows, rows]
            + [pl.BlockSpec((3, 8, LANES), lambda i: (0, 0, chunk + i))] * (not in_parts)
            + [pl.BlockSpec((3, 3, LANES), lambda i: (0, 0, chunk + i))]
            + [whole_block((1, tok_count))] * len(filters),
            out_specs=out_specs,
            out_shape=out_shape,
            scratch_shapes=[pltpu.VMEM((tok_count, LANES), jnp.float32), pltpu.VMEM((3, 8 + B, LANES), jnp.float32)]
            + [pltpu.VMEM((slabs, B), jnp.float32)] * in_parts,
            compiler_params=params(),
            cost_estimate=cost(count * 40 * tok_count * LANES, count * 6 * tok_count * LANES),
            name="pre",
        )(key_proj, value_proj, *[halo] * (not in_parts), short_taps, *filters)

    def conv(start, first, count, coded, *scale):
        rows = A * per
        args = (coded, *scale, left, right, turn_re, turn_im, spec_re, spec_im)
        in_specs = [whole_block(arg.shape) for arg in args]
        scratch = [pltpu.VMEM((2, rows, LANES), jnp.float32)]
        if in_parts:
            args = (place, coded, short_taps) + args[1:]
            block = (seq_count, 1, coded.shape[2], B)
            in_specs = [SCALAR, pl.BlockSpec(block, lambda i: (0, first + i, 0, 0))]
            in_specs.append(pl.BlockSpec((3, 3, LANES), lambda i: (0, 0, start + i)))
            in_specs += [pl.BlockSpec(memory_space=pltpu.HBM)] * 6
            out_shape = [jax.ShapeDtypeStruct((seq_count, count, size, B), jnp.bfloat16)]
            out_specs = [pl.BlockSpec((seq_count, 1, size, B), lambda i: (0, i, 0, 0))]
            scratch += [pltpu.VMEM((A, LANES), jnp.float32), pltpu.VMEM((LANES, LANES), jnp.float32)]
            scratch += [pltpu.VMEM(arg.shape, arg.dtype) for arg in args[3:]] + [pltpu.SemaphoreType.DMA((6,))]
        else:
            out_shape = [
                jax.ShapeDtypeStruct((rows, B), jnp.bfloat16),
                jax.ShapeDtypeStruct((8, LANES), jnp.float32),
            ]
            out_specs = [whole_block(out.shape) for out in out_shape]
        return pl.pallas_call(
            partial(conv_parts_kernel, per) if in_parts else conv_whole_kernel,
            grid=(count,),
            in_specs=in_specs,
            out_specs=out_specs,
            out_shape=out_shape,
            scratch_shapes=scratch,
            compiler_params=params(),
            cost_estimate=cost(count * per // 2 * 4 * 2 * 512 * 1536 * 256, count * 4 * rows * B),
            name="conv",
        )(*args)

    def post(chunk, count, out, coded, *scale):
        step = min(2048, tok_count)
        block = step // B
        rows = pl.BlockSpec((step, LANES), lambda u, i: (i, chunk + u))
        in_specs = [
            rows,
            rows,
            rows,
            pl.BlockSpec((3, 8, LANES), lambda u, i: (0, 0, chunk + u)),
            pl.BlockSpec((3, 3, LANES), lambda u, i: (0, 0, chunk + u)),
            pl.BlockSpec((1, LANES), lambda u, i: (0, chunk + u)),
        ]
        args = [query_proj, key_proj, value_proj, halo, short_taps, skip_row]
        if in_parts:
            last = slabs * per // EXTRA
            in_specs += [
                pl.BlockSpec((seq_count, 1, block * per, B), lambda u, i: (0, u, i, 0)),
                pl.BlockSpec((seq_count, 1, EXTRA, B), lambda u, i: (0, u, last, 0)),
            ]
            args += [coded, coded]
        else:
            in_specs += [
                pl.BlockSpec((block, LANES, B), lambda u, i: (i, 0, 0)),
                pl.BlockSpec((1, LANES), lambda u, i: (0, 0)),
            ]
            args += [coded, *scale]
        if out is not None:
            in_specs.append(pl.BlockSpec(memory_space=pl.ANY))
            args.append(out)
        return pl.pallas_call(
            post_parts_kernel if in_parts else post_whole_kernel,
            grid=(count, tok_count // step),
            in_specs=in_specs,
            out_specs=rows,
            out_shape=jax.ShapeDtypeStruct((tok_count, chan_width), jnp.float32),
            scratch_shapes=[pltpu.VMEM((3, 8 + B, LANES), jnp.float32)],
            input_output_aliases={} if out is None else {len(args) - 1: 0},
            compiler_params=params(),
            cost_estimate=cost(count * 60 * tok_count * LANES, count * 12 * tok_count * LANES),
            name="post",
        )(*args)

    if in_parts:
        arrived = [(0, swap(*pre(0, 1, long_filter)))]
        if chunks > 1:
            arrived.append((1, swap(*pre(1, chunks - 1))))
        whole_filter = arrived[0][1]
        filter_spec = pl.BlockSpec((seq_count, 1, 2 * slabs, B), lambda i: (0, 0, per // 2, 0))
    else:
        whole_filter = swap(jnp.broadcast_to(long_filter.reshape(slabs, B), (seq_count, slabs, B))).reshape(A, B)
        filter_spec = whole_block((A, B))
    cos_hi, sin_hi, cos_lo, sin_lo, turn_re, turn_im = (jnp.asarray(table) for table in tables())
    filter_args = (whole_filter, cos_hi, sin_hi, cos_lo, sin_lo, turn_re, turn_im)
    spec_shape = [jax.ShapeDtypeStruct((A, B), jnp.float32)] * 2
    spec_shape += [jax.ShapeDtypeStruct((2 * A, 3 * A), jnp.bfloat16), jax.ShapeDtypeStruct((6 * B, 2 * B), jnp.bfloat16)]
    spec_re, spec_im, left, right = pl.pallas_call(
        parts_spectrum_kernel if in_parts else spectrum_kernel,
        grid=(1,),
        in_specs=[filter_spec] + [whole_block((A, B))] * 6,
        out_specs=[whole_block(out.shape) for out in spec_shape],
        out_shape=spec_shape,
        scratch_shapes=[pltpu.VMEM((A, B), jnp.float32)] * in_parts,
        compiler_params=params(),
        cost_estimate=cost(2 * 2 * 512 * 1536 * 256, 16 * A * B),
        name="spectrum",
    )(*filter_args)

    out = None
    if in_parts:
        cuts = sorted({0, 1, chunks - 1, chunks})
        returned = []
        for start, stop in zip(cuts[:-1], cuts[1:]):
            source, coded = arrived[min(start, 1)]
            (coded,) = conv(start, start - source, stop - start, coded)
            if start == 0:
                coded, halo = lax.optimization_barrier((coded, halo))
            returned.append((start, stop - start, swap(coded)))
        for start, count, coded in returned:
            out = post(start, count, out, coded)
    else:
        returned = []
        for chunk in range(chunks):
            coded, scale = pre(chunk, 1)
            coded = swap(coded.reshape(slabs, seq_count, per, B).transpose(1, 0, 2, 3))
            scale = jnp.repeat(swap(scale.reshape(seq_count, per)), slabs, axis=0)
            scale = jnp.pad(scale, ((0, 0), (0, LANES - per)))
            coded, scale = conv(chunk, 0, 1, coded.reshape(A * per, B), scale)
            coded = swap(coded.reshape(seq_count, slabs, per, B))
            scale = lax.all_gather(scale[0, :per], "seq", axis=0, tiled=True)
            returned.append((coded.transpose(1, 0, 2, 3).reshape(slabs, LANES, B), scale.reshape(1, LANES)))
        for chunk, (coded, scale) in enumerate(returned):
            out = post(chunk, 1, out, coded, scale)
    return out


def solution(mesh):
    return jax.shard_map(
        per_device,
        mesh=mesh,
        in_specs=(
            P("seq", "chan"),
            P("seq", "chan"),
            P("seq", "chan"),
            P(None, None, "chan"),
            P("chan"),
            P("chan", "seq"),
        ),
        out_specs=P("seq", "chan"),
        check_vma=False,
    )
```
